256 devices in a mesh: grp: 4 (over z_lo, core), tp: 64 (over y, x, z_hi).
Axes of the slice: x: 4, y: 4, z: 8 (z_hi: 4, z_lo: 2; z = z_hi * 2 + z_lo), core: 2. Of those that a mesh axis runs over, the one named last changes fastest.
Arguments:
- hidden: bfloat16 [32768, 1024], P(('grp', 'tp')), may hold values from -6 to 6
- ln_gain: bfloat16 [1024], replicated, may hold values from 0.5 to 1.5
- w_query: bfloat16 [1024, 1024], replicated, may hold values from -0.1875 to 0.1875
- w_key: bfloat16 [1024, 1024], replicated, may hold values from -0.1875 to 0.1875
- w_value: bfloat16 [1024, 1024], replicated, may hold values from -0.1875 to 0.1875
- w_out: bfloat16 [1024, 1024], replicated, may hold values from -0.1875 to 0.1875
- rel_bias: float32 [32, 16], replicated, may hold values from -8 to 8
- prefix_cache: bfloat16 [8, 512, 2, 1024], P('grp', 'tp'), may hold values from -14 to 14
- bucket_of_distance: int32 [1024], replicated, may hold values from 0 to 31, never falling along the last dimension, each value on 1 to 256 neighbouring positions
- slot_of_group: int32 [8], replicated, may hold values from 0 to 7, each once
- suffix_lengths: int32 [4, 128], P('grp'), may hold values from 1 to 512, 8192 in all within a row
- request_group: int32 [4, 128], P('grp'), may hold values from 0 to 1
Outputs:
- attended: bfloat16 [32768, 1024], P(('grp', 'tp'))
The draws below stay inside these ranges and needn't reach their ends.
Inputs may be any that keep to these rules, and one draw needn't show every extreme that they name: `suffix_lengths`: each row's lengths sum to 8192; the longest is exactly 512. `slot_of_group`: every slot holds exactly one group. `bucket_of_distance`: never falls with the distance; bucket 0 starts at distance 0.
All inputs are finite; a program needn't handle non-finite values.
Results may differ from the reference program's by a relative error of at most 0.005.
The reference program's roundings to bfloat16 on the way count: a program that leaves them out, or rounds other values in their place, can miss the bound.
Values may be sent and summed in bfloat16 or wider, within the bound.
A program may use at most 192 MiB of HBM per device.

```python
import math
import jax
import jax.numpy as jnp
import numpy as np
from jax import lax

D = 1024
H = 16
NB = 32
DH = 64
PREFIX = 512
GRP_SLOTS = 2
TOK_DEV = 128
LMAX = 512
SPAN = 1024
BUCKET_MOST = 256
ROW_TOK = 8192
TOKENS = 32768
GROUPS = 8
REQ_ROW = 128
N_GRP = 4
N_TP = 64


def draw_prefix_cache(key, part):
    shape = (GROUPS, PREFIX, 2, D)
    first = jax.random.fold_in(key, 0)
    return jnp.clip(jax.random.normal(first, shape, jnp.float32), -6.0, 6.0).astype(jnp.bfloat16)


def touch_ends(values, stream_key, low, largest):
    longest = values.shape.index(max(values.shape))
    spots = []
    for shift in (0, 1):
        where = [jax.random.randint(jax.random.fold_in(stream_key, axis), (), 0, length) for axis, length in enumerate(values.shape)]
        where[longest] = (where[longest] + shift) % values.shape[longest]
        spots.append(tuple(where))
    return values.at[spots[0]].set(low).at[spots[1]].set(largest)


def block_levels(own_key, extent, shards, smallest, high):
    loudness = 1.0
    for position, parts in shards:
        draws = jax.random.uniform(jax.random.fold_in(jax.random.fold_in(own_key, 6), position), (parts,), jnp.float32, smallest / len(shards), high / len(shards))
        loudness = loudness * jnp.repeat(jnp.exp(draws), extent[position] // parts).reshape((-1,) + (1,) * (len(extent) - 1 - position))
    return loudness


def length_profile(count, total, bound, lean):
    portions = [(1 << 20) // math.isqrt(rank ** lean) + 1 for rank in range(2, count + 1)]
    spare, counts = total - bound - (count - 1), [1] * (count - 1)
    while spare > 0:
        candidates = [i for i in range(count - 1) if counts[i] < bound]
        whole, remaining = sum([portions[i] for i in candidates]), spare
        for i in candidates:
            addition = min(bound - counts[i], max(1, remaining * portions[i] // whole), spare)
            counts[i] = counts[i] + addition
            spare = spare - addition
    return np.array([bound] + counts)


def uneven_parts(rng, amount, total, bound, lean):
    if amount == 2:
        one = jax.random.randint(rng, (), max(1, total - bound), min(bound, total - 1) + 1)
        return jnp.stack([one, total - one])
    sizes = jnp.asarray(length_profile(amount, total, bound, lean), jnp.int32)
    pairs = (amount - 1) // 2
    donor, sink = sizes[1:1 + 2 * pairs:2], sizes[2:2 + 2 * pairs:2]
    room = jnp.minimum(donor - 1, bound - sink)
    shifted = jax.random.randint(jax.random.fold_in(rng, 1), (pairs,), 0, 1 << 20) % (room + 1)
    sizes = sizes.at[1:1 + 2 * pairs:2].set(donor - shifted).at[2:2 + 2 * pairs:2].set(sink + shifted)
    return sizes[jax.random.permutation(jax.random.fold_in(rng, 2), amount)]


def noise(rng, extent, spread, reach, cuts=(), held_as=jnp.bfloat16):
    gain = block_levels(rng, extent, cuts, -0.22, 0.18) if cuts else 1.0
    result = jax.random.normal(rng, extent, jnp.float32) * spread * gain
    return jnp.minimum(jnp.maximum(result, -reach), reach).astype(held_as)


def setup_inputs(seed: int = 0) -> dict:
    key_list = jax.random.split(jax.random.key(seed), 13)
    return {
        "hidden": noise(key_list[0], (TOKENS, D), 1.0, 6.0, ((0, 256),)),
        "ln_gain": jnp.clip(1.0 + 0.1 * jax.random.normal(key_list[1], (D,), jnp.float32), 0.5, 1.5).astype(jnp.bfloat16),
        "w_query": noise(key_list[2], (D, D), D ** -0.5, 0.1875),
        "w_key": noise(key_list[3], (D, D), D ** -0.5, 0.1875),
        "w_value": noise(key_list[4], (D, D), D ** -0.5, 0.1875),
        "w_out": noise(key_list[5], (D, D), D ** -0.5, 0.1875),
        "rel_bias": noise(key_list[6], (NB, H), 2.0, 8.0, (), jnp.float32),
        "prefix_cache": draw_prefix_cache(jax.random.fold_in(key_list[12], 71), 0),
        "bucket_of_distance": jnp.searchsorted(jnp.cumsum(uneven_parts(key_list[8], NB, SPAN, BUCKET_MOST, 2)), jnp.arange(SPAN), side="right").astype(jnp.int32),
        "slot_of_group": jax.random.permutation(key_list[9], GROUPS).astype(jnp.int32),
        "suffix_lengths": jax.vmap(lambda own: uneven_parts(own, REQ_ROW, ROW_TOK, LMAX, 2))(jax.random.split(key_list[10], N_GRP)).reshape((N_GRP, REQ_ROW)).astype(jnp.int32),
        "request_group": touch_ends(jax.random.randint(key_list[11], (N_GRP, REQ_ROW), 0, GRP_SLOTS), jax.random.fold_in(key_list[11], 1), 0, GRP_SLOTS - 1).astype(jnp.int32),
    }


def request_meta(lens, rows):
    ends = jnp.cumsum(lens).astype(jnp.int32)
    starts = (ends - lens).astype(jnp.int32)
    count = lens.shape[0]
    req = lax.optimization_barrier(jnp.sum((rows[:, None] >= ends[None, :]).astype(jnp.int32), axis=1)).astype(jnp.int32)
    req = jnp.minimum(req, count - 1)
    onehot = req[:, None] == jnp.arange(count).astype(jnp.int32)[None, :]
    start_of = lax.optimization_barrier(jnp.sum(jnp.where(onehot, starts[None, :], 0), axis=1)).astype(jnp.int32)
    return (req, (rows - start_of).astype(jnp.int32), onehot)

def reference(hidden, ln_gain, w_query, w_key, w_value, w_out, rel_bias, prefix_cache, bucket_of_distance, slot_of_group, suffix_lengths, request_group):
    x = hidden.astype(jnp.float32)
    normed = (x * lax.rsqrt(lax.optimization_barrier(jnp.mean(x * x, axis=1, keepdims=True)) + 1e-06) * ln_gain.astype(jnp.float32)).astype(jnp.bfloat16)
    query = jnp.dot(normed, w_query, preferred_element_type=jnp.float32).astype(jnp.bfloat16)
    key = jnp.dot(normed, w_key, preferred_element_type=jnp.float32).astype(jnp.bfloat16)
    value = jnp.dot(normed, w_value, preferred_element_type=jnp.float32).astype(jnp.bfloat16)
    table = jnp.dot(jax.nn.one_hot(bucket_of_distance, NB, dtype=jnp.float32), rel_bias, precision=lax.Precision.HIGHEST)
    pieces = []
    for row in range(N_GRP):
        low = row * ROW_TOK
        q_row = query[low:low + ROW_TOK]
        lens = suffix_lengths[row]
        groups = request_group[row]
        rows = jnp.arange(ROW_TOK).astype(jnp.int32)
        req, pos, onehot = request_meta(lens, rows)
        grp_of = lax.optimization_barrier(jnp.sum(jnp.where(onehot, groups[None, :], 0), axis=1)).astype(jnp.int32)
        slots = slot_of_group[row * GRP_SLOTS:(row + 1) * GRP_SLOTS]
        chosen = prefix_cache[slots].astype(jnp.float32)
        k_pad = jnp.concatenate([jnp.zeros((LMAX, D), jnp.bfloat16), key[low:low + ROW_TOK]], axis=0)
        v_pad = jnp.concatenate([jnp.zeros((LMAX, D), jnp.bfloat16), value[low:low + ROW_TOK]], axis=0)
        req_pad = jnp.concatenate([jnp.full((LMAX,), -1, jnp.int32), req], axis=0)
        pos_pad = jnp.concatenate([jnp.zeros((LMAX,), jnp.int32), pos], axis=0)
        prefix_pos = jnp.arange(PREFIX).astype(jnp.int32)

        def block(index):
            start = (index * TOK_DEV).astype(jnp.int32)
            qh = lax.dynamic_slice_in_dim(q_row, start, TOK_DEV, 0).astype(jnp.float32).reshape(TOK_DEV, H, DH)
            kh = lax.dynamic_slice_in_dim(k_pad, start, LMAX + TOK_DEV, 0).astype(jnp.float32).reshape(LMAX + TOK_DEV, H, DH)
            vh = lax.dynamic_slice_in_dim(v_pad, start, LMAX + TOK_DEV, 0).astype(jnp.float32).reshape(LMAX + TOK_DEV, H, DH)
            rq = lax.dynamic_slice_in_dim(req, start, TOK_DEV, 0)
            pq = lax.dynamic_slice_in_dim(pos, start, TOK_DEV, 0)
            gq = lax.dynamic_slice_in_dim(grp_of, start, TOK_DEV, 0)
            rk = lax.dynamic_slice_in_dim(req_pad, start, LMAX + TOK_DEV, 0)
            pk = lax.dynamic_slice_in_dim(pos_pad, start, LMAX + TOK_DEV, 0)
            dist = jnp.clip(pq[:, None] - pk[None, :], 0, SPAN - 1)
            s_suf = jnp.einsum('qhd,khd->qhk', qh, kh) + jnp.take(table, dist, axis=0).transpose(0, 2, 1)
            valid = (rq[:, None] == rk[None, :]) & (pk[None, :] <= pq[:, None])
            s_suf = jnp.where(valid[:, None, :], s_suf, -jnp.inf)
            dist_pre = PREFIX + pq[:, None] - prefix_pos[None, :]
            s_pre = jnp.zeros((TOK_DEV, H, PREFIX), jnp.float32)
            for slot in range(GRP_SLOTS):
                s_one = jnp.einsum('qhd,khd->qhk', qh, chosen[slot, :, 0].reshape(PREFIX, H, DH))
                s_pre = jnp.where((gq == slot)[:, None, None], s_one, s_pre)
            s_pre = s_pre + jnp.take(table, dist_pre, axis=0).transpose(0, 2, 1)
            top = jnp.maximum(lax.optimization_barrier(jnp.max(s_suf, axis=-1)), lax.optimization_barrier(jnp.max(s_pre, axis=-1)))
            p_suf = jnp.exp(s_suf - top[..., None])
            p_pre = jnp.exp(s_pre - top[..., None])
            total = lax.optimization_barrier(jnp.sum(p_suf, axis=-1)) + lax.optimization_barrier(jnp.sum(p_pre, axis=-1))
            b_suf = lax.optimization_barrier(p_suf.astype(jnp.bfloat16)).astype(jnp.float32)
            b_pre = lax.optimization_barrier(p_pre.astype(jnp.bfloat16)).astype(jnp.float32)
            mixed = jnp.einsum('qhk,khd->qhd', b_suf, vh)
            for slot in range(GRP_SLOTS):
                picked = jnp.where((gq == slot)[:, None, None], b_pre, 0.0)
                mixed = mixed + jnp.einsum('qhk,khd->qhd', picked, chosen[slot, :, 1].reshape(PREFIX, H, DH))
            return (mixed / total[..., None]).reshape(TOK_DEV, D).astype(jnp.bfloat16)
        pieces.append(lax.map(block, jnp.arange(N_TP).astype(jnp.int32)).reshape(ROW_TOK, D))
    mixed_all = jnp.concatenate(pieces, axis=0)
    return jnp.dot(mixed_all, w_out, preferred_element_type=jnp.float32).astype(jnp.bfloat16)
```

```python
import jax
import jax.numpy as jnp
from jax import lax
from jax.experimental import pallas as pl
from jax.experimental.pallas import tpu as pltpu
from jax.sharding import PartitionSpec as P

D = 1024
H = 16
TOK = 128
LMAX = 512
KEYS = LMAX + TOK
PREFIX = 512
SPAN = 1024
NEG = -1e30


def attend_kernel(
    pos_ref,
    hid_ref,
    gain_ref,
    wq_ref,
    wk_ref,
    wv_ref,
    wo_ref,
    rt_ref,
    grp_ref,
    pk_ref,
    pv_ref,
    out_ref,
    n_ref,
    q_ref,
    k_ref,
    v_ref,
    b_ref,
    mix_ref,
):
    f32 = jnp.float32
    bf16 = jnp.bfloat16
    gain = gain_ref[...].astype(f32)

    def norm(i, _):
        rows = pl.ds(pl.multiple_of(i * TOK, TOK), TOK)
        x = hid_ref[rows, :].astype(f32)
        ms = jnp.mean(x * x, axis=1, keepdims=True)
        n_ref[rows, :] = (x * lax.rsqrt(ms + 1e-06) * gain).astype(bf16)
        return 0

    lax.fori_loop(0, KEYS // TOK, norm, 0)

    def project(i, _):
        cols = pl.ds(pl.multiple_of(i * 256, 256), 256)
        q_ref[:, cols] = jnp.dot(
            n_ref[pl.ds(LMAX, TOK), :], wq_ref[:, cols], preferred_element_type=f32
        ).astype(bf16)
        k_ref[:, cols] = jnp.dot(n_ref[...], wk_ref[:, cols], preferred_element_type=f32).astype(
            bf16
        )
        v_ref[:, cols] = jnp.dot(n_ref[...], wv_ref[:, cols], preferred_element_type=f32).astype(
            bf16
        )
        return 0

    lax.fori_loop(0, D // 256, project, 0)

    lane = lax.broadcasted_iota(jnp.int32, (H, 128), 1)

    def bias(a, _):
        pos = pos_ref[a]
        rows = pl.ds(pl.multiple_of(a * H, H), H)
        off = PREFIX - 1 - pos
        base = lax.shift_right_logical(off, 7)
        keep = 128 - jnp.bitwise_and(off, 127)
        turn = jnp.bitwise_and(keep, 127)
        tiles = [
            pltpu.roll(rt_ref[:, pl.ds(pl.multiple_of((base + j) * 128, 128), 128)], turn, 1)
            for j in range(5)
        ]
        for j in range(4):
            b_ref[5 + j, rows, :] = jnp.where(
                lane < keep, tiles[j], tiles[j + 1]
            )
        turn = jnp.bitwise_and(a + 1, 127)
        tiles = [pltpu.roll(rt_ref[:, 384 + 128 * j : 512 + 128 * j], turn, 1) for j in range(6)]
        low = LMAX + a - pos
        for j in range(5):
            col = lane + 128 * j
            good = (col >= low) & (col <= LMAX + a)
            b_ref[j, rows, :] = jnp.where(
                good, jnp.where(lane < a + 1, tiles[j], tiles[j + 1]), NEG
            )
        return 0

    lax.fori_loop(0, TOK, bias, 0)

    first = grp_ref[...] == 0
    first2 = jnp.concatenate([first, first], axis=0)
    half = lax.broadcasted_iota(jnp.int32, (TOK, 128), 1) < 64
    nt = (((1,), (1,)), ((), ()))

    def heads(p, _):
        cols = pl.ds(pl.multiple_of(p * 128, 128), 128)
        q = q_ref[:, cols].astype(f32)
        qq = jnp.concatenate([jnp.where(half, q, 0.0), jnp.where(half, 0.0, q)], axis=0)
        qg = jnp.concatenate(
            [jnp.where(first2, qq, 0.0), jnp.where(first2, 0.0, qq)], axis=1
        ).astype(bf16)
        kcat = jnp.concatenate(
            [pk_ref[:, s, :, cols].reshape(PREFIX, 128) for s in range(2)], axis=1
        )
        vcat = jnp.concatenate(
            [pv_ref[:, s, :, cols].reshape(PREFIX, 128) for s in range(2)], axis=1
        )
        bias2 = jnp.concatenate(
            [
                jnp.concatenate(
                    [b_ref[j, pl.ds(2 * p + e, TOK, stride=H), :] for j in range(9)], axis=1
                )
                for e in range(2)
            ],
            axis=0,
        )
        suf = (
            lax.dot_general(qq.astype(bf16), k_ref[:, cols], nt, preferred_element_type=f32)
            + bias2[:, :KEYS]
        )
        pre = lax.dot_general(qg, kcat, nt, preferred_element_type=f32) + bias2[:, KEYS:]
        top = jnp.maximum(
            jnp.max(suf, axis=1, keepdims=True), jnp.max(pre, axis=1, keepdims=True)
        )
        esuf = jnp.exp(suf - top)
        epre = jnp.exp(pre - top)
        total = jnp.sum(esuf, axis=1, keepdims=True) + jnp.sum(epre, axis=1, keepdims=True)
        osuf = jnp.dot(esuf.astype(bf16), v_ref[:, cols], preferred_element_type=f32)
        opre = jnp.dot(epre.astype(bf16), vcat, preferred_element_type=f32)
        o = (osuf + jnp.where(first2, opre[:, :128], opre[:, 128:])) / total
        mix_ref[:, cols] = jnp.where(half, o[:TOK], o[TOK:]).astype(bf16)
        return 0

    lax.fori_loop(0, H // 2, heads, 0)

    out_ref[...] = jnp.dot(mix_ref[...], wo_ref[...], preferred_element_type=f32).astype(bf16)


def attend(pos, hid, gain, wq, wk, wv, wo, rt, grp, pk, pv):
    vmem = pl.BlockSpec(memory_space=pltpu.VMEM)
    return pl.pallas_call(
        attend_kernel,
        out_shape=jax.ShapeDtypeStruct((TOK, D), jnp.bfloat16),
        in_specs=[pl.BlockSpec(memory_space=pltpu.SMEM)] + [vmem] * 10,
        out_specs=vmem,
        scratch_shapes=[
            pltpu.VMEM((KEYS, D), jnp.bfloat16),
            pltpu.VMEM((TOK, D), jnp.bfloat16),
            pltpu.VMEM((KEYS, D), jnp.bfloat16),
            pltpu.VMEM((KEYS, D), jnp.bfloat16),
            pltpu.VMEM(((KEYS + PREFIX) // 128, TOK * H, 128), jnp.float32),
            pltpu.VMEM((TOK, D), jnp.bfloat16),
        ],
        compiler_params=pltpu.CompilerParams(vmem_limit_bytes=56 << 20),
        name="attend",
    )(pos, hid, gain, wq, wk, wv, wo, rt, grp, pk, pv)


def shifted(array, axis, by):
    peers = lax.axis_size(axis)
    pairs = [(i, i + by) for i in range(peers) if 0 <= i + by < peers]
    return lax.ppermute(array, axis, pairs)


def shards(
    hidden,
    ln_gain,
    w_query,
    w_key,
    w_value,
    w_out,
    rel_bias,
    prefix_cache,
    bucket_of_distance,
    slot_of_group,
    suffix_lengths,
    request_group,
):
    tp_index = lax.axis_index("tp")
    row_index = lax.axis_index("grp")
    earlier = [shifted(hidden, "tp", step) for step in range(LMAX // TOK, 0, -1)]
    hid = jnp.concatenate(earlier + [hidden], axis=0)

    row_slots = lax.dynamic_slice_in_dim(slot_of_group, row_index * 2, 2)
    owners = lax.all_gather(prefix_cache, "grp", axis=0, tiled=True)
    mine = jnp.take(owners, row_slots, axis=0)
    kv = lax.all_gather(mine, "tp", axis=1, tiled=True)
    kv = kv.reshape(2, 16, 32, 2, D)
    pk = kv[:, :, :, 0].transpose(1, 0, 2, 3)
    pv = kv[:, :, :, 1].transpose(1, 0, 2, 3)

    lens = suffix_lengths[0]
    ends = jnp.cumsum(lens)
    starts = ends - lens
    rows = tp_index * TOK + jnp.arange(TOK)
    req = jnp.minimum(jnp.sum((rows[:, None] >= ends[None, :]).astype(jnp.int32), axis=1), 127)
    onehot = req[:, None] == jnp.arange(lens.shape[0])[None, :]
    pos = rows - jnp.sum(jnp.where(onehot, starts[None, :], 0), axis=1)
    grp = jnp.sum(jnp.where(onehot, request_group[0][None, :], 0), axis=1)

    table = jnp.dot(
        rel_bias.T,
        jax.nn.one_hot(bucket_of_distance[::-1], rel_bias.shape[0], dtype=jnp.float32, axis=0),
        precision=lax.Precision.HIGHEST,
    )
    rt = jnp.pad(table, ((0, 0), (0, 128)))
    return attend(
        pos, hid, ln_gain[None, :], w_query, w_key, w_value, w_out, rt, grp[:, None], pk, pv
    )


def solution(mesh):
    in_specs = (
        P(("grp", "tp"), None),
        P(),
        P(),
        P(),
        P(),
        P(),
        P(),
        P("grp", "tp", None, None),
        P(),
        P(),
        P("grp", None),
        P("grp", None),
    )
    out_specs = P(("grp", "tp"), None)
    return jax.shard_map(shards, mesh=mesh, in_specs=in_specs, out_specs=out_specs, check_vma=False)
```

```python
import jax
import jax.numpy as jnp
from jax import lax
from jax.experimental import pallas as pl
from jax.experimental.pallas import tpu as pltpu
from jax.sharding import PartitionSpec as P

D = 1024
H = 16
TOK = 128
LMAX = 512
KEYS = LMAX + TOK
PREFIX = 512
SPAN = 1024
NEG = -1e30
MESH = pl.DeviceIdType.MESH


def layer_kernel(
    pos_ref,
    slot_ref,
    hid_ref,
    pre_ref,
    gain_ref,
    rt_ref,
    grp_ref,
    place_ref,
    wq_hbm,
    wk_hbm,
    wv_hbm,
    wo_hbm,
    out_ref,
    wq_ref,
    wk_ref,
    wv_ref,
    wo_ref,
    own_ref,
    z_ref,
    all_ref,
    pk_ref,
    pv_ref,
    n_ref,
    q_ref,
    k_ref,
    v_ref,
    s_ref,
    b_ref,
    mask_ref,
    mix_ref,
    send_sem,
    recv_sem,
    load_sem,
):
    f32 = jnp.float32
    bf16 = jnp.bfloat16
    g = lax.axis_index("grp")
    t = lax.axis_index("tp")
    y, x, z = t // 16, (t // 4) % 4, t % 4

    def tp_id(i):
        return (g, lax.rem(i + 128, 64))

    def z_id(d):
        return (g, y * 16 + x * 4 + lax.rem(z + d + 4, 4))

    def x_id(d):
        return (g, y * 16 + lax.rem(x + d + 4, 4) * 4 + z)

    def y_id(d):
        return (g, lax.rem(y + d + 4, 4) * 16 + x * 4 + z)

    used = []

    def copy(src, dst, device):
        i = len(used)
        out = pltpu.make_async_remote_copy(
            src_ref=src,
            dst_ref=dst,
            send_sem=send_sem.at[i],
            recv_sem=recv_sem.at[i],
            device_id=device,
            device_id_type=MESH,
        )
        out.start()
        used.append(out)
        return out

    loads = [
        pltpu.make_async_copy(src, dst, load_sem.at[i])
        for i, (src, dst) in enumerate(
            [(wq_hbm, wq_ref), (wk_hbm, wk_ref), (wv_hbm, wv_ref), (wo_hbm, wo_ref)]
        )
    ]
    for load in loads:
        load.start()

    row_ids = [(lax.rem(g + d, 4), t) for d in (1, 2, 3)]
    greet = row_ids + [tp_id(t + d) for d in (1, -1, 4, -4)]
    greet = greet + [ring(d) for ring in (x_id, y_id, z_id) for d in (1, -1)]
    barrier = pltpu.get_barrier_semaphore()
    for device in greet:
        pl.semaphore_signal(barrier, inc=1, device_id=device, device_id_type=MESH)
    pl.semaphore_wait(barrier, len(greet))

    own_ref[pl.ds(2 * g, 2)] = pre_ref[...]
    rows = [copy(pre_ref, own_ref.at[pl.ds(2 * g, 2)], device) for device in row_ids]
    block = [all_ref.at[pl.ds(TOK * i, TOK)] for i in range(4)]
    back4 = copy(hid_ref, block[0], tp_id(t + 4))
    for c in rows:
        c.wait_recv()
    for s in range(2):
        slot = jnp.full((8, 2 * D), slot_ref[2 * g + s], jnp.int32)
        chosen = own_ref[0].astype(f32)
        for i in range(1, 8):
            chosen = jnp.where(slot == i, own_ref[i].astype(f32), chosen)
        z_ref[z, s] = chosen.astype(bf16)

    def spread(buf, piece, me, ring):
        part = buf.at[piece(me)]
        return [copy(part, part, ring(1)), copy(part, part, ring(-1))]

    def onward(buf, piece, me, ring, first, step):
        first[0 if step == 1 else 1].wait_recv()
        part = buf.at[piece(lax.rem(me - step + 4, 4))]
        return copy(part, part, ring(step))

    zs = [spread(z_ref, lambda i, s=s: (i, s), z, z_id) for s in range(2)]
    back1 = copy(hid_ref, block[3], tp_id(t + 1))
    zfwd = [
        onward(z_ref, lambda i, s=s: (i, s), z, z_id, zs[s], 1 - 2 * s) for s in range(2)
    ]
    back4.wait_recv()
    back3 = copy(block[0], block[1], tp_id(t - 1))
    zs[0][1].wait_recv()
    zs[1][0].wait_recv()
    for c in zfwd:
        c.wait_recv()

    for s in range(2):
        for i in range(2):
            both = jnp.concatenate(
                [z_ref[2 * i, s].astype(f32), z_ref[2 * i + 1, s].astype(f32)], axis=0
            ).astype(bf16)
            pk_ref[y * 4 + x, s, 16 * i : 16 * (i + 1), :] = both[:, :D]
            pv_ref[y * 4 + x, s, 16 * i : 16 * (i + 1), :] = both[:, D:]

    def at_x(i, other, s):
        return (other * 4 + i, s)

    def at_y(i, other, s):
        return (i * 4 + other, s)

    lines = []
    for s in range(2):
        lines.append((pk_ref, s, x, y, x_id, y_id, at_x, at_y))
        lines.append((pv_ref, s, y, x, y_id, x_id, at_y, at_x))
    one = []
    for buf, s, me, other, ring, _, at, _ in lines:
        one.append(spread(buf, lambda i, s=s, at=at, o=other: at(i, o, s), me, ring))

    def second(line, shift):
        buf, s, me, other, _, ring, _, at = line
        chunk = lax.rem(me + shift + 4, 4)
        return spread(buf, lambda i: at(i, chunk, s), other, ring)

    def second_on(line, shift, first):
        buf, s, me, other, _, ring, _, at = line
        chunk = lax.rem(me + shift + 4, 4)
        step = 1 - 2 * s
        return onward(buf, lambda i: at(i, chunk, s), other, ring, first, step)

    two = [{0: second(line, 0)} for line in lines]
    far = []
    for line, first, rest in zip(lines, one, two):
        buf, s, me, other, ring, _, at, _ = line
        step = 1 - 2 * s
        far.append(onward(buf, lambda i: at(i, other, s), me, ring, first, step))
        rest[-step] = second(line, -step)
    for line, first, rest in zip(lines, one, two):
        step = 1 - 2 * line[1]
        first[1 if step == 1 else 0].wait_recv()
        rest[step] = second(line, step)

    back1.wait_recv()
    low = pl.ds(TOK * 2, TOK // 2)
    high = pl.ds(TOK * 2 + TOK // 2, TOK // 2)
    back2a = copy(all_ref.at[pl.ds(TOK * 3, TOK // 2)], all_ref.at[low], tp_id(t + 1))
    back3.wait_recv()
    back2b = copy(
        all_ref.at[pl.ds(TOK + TOK // 2, TOK // 2)], all_ref.at[high], tp_id(t - 1)
    )

    last = [second_on(line, 0, rest[0]) for line, rest in zip(lines, two)]
    for line, rest, c in zip(lines, two, far):
        c.wait_recv()
        rest[2] = second(line, 2)
    for shift in (1, -1, 2):
        last = last + [
            second_on(line, shift, rest[shift]) for line, rest in zip(lines, two)
        ]
    for line, rest in zip(lines, two):
        step = 1 - 2 * line[1]
        for shift in (0, 1, -1, 2):
            rest[shift][1 if step == 1 else 0].wait_recv()
    for c in last:
        c.wait_recv()
    back2a.wait_recv()
    back2b.wait_recv()
    for c in used:
        c.wait_send()

    all_ref[pl.ds(LMAX, TOK)] = hid_ref[...]
    for load in loads:
        load.wait()

    gain = gain_ref[...].astype(f32)

    def norm(i, _):
        rows = pl.ds(pl.multiple_of(i * TOK, TOK), TOK)
        x = all_ref[rows, :].astype(f32)
        ms = jnp.mean(x * x, axis=1, keepdims=True)
        n_ref[rows, :] = (x * lax.rsqrt(ms + 1e-06) * gain).astype(bf16)
        return 0

    lax.fori_loop(0, KEYS // TOK, norm, 0)

    def project(i, _):
        cols = pl.ds(pl.multiple_of(i * 256, 256), 256)
        q_ref[:, cols] = jnp.dot(
            n_ref[pl.ds(LMAX, TOK), :], wq_ref[:, cols], preferred_element_type=f32
        ).astype(bf16)
        k_ref[:, cols] = jnp.dot(n_ref[...], wk_ref[:, cols], preferred_element_type=f32).astype(
            bf16
        )
        v_ref[:, cols] = jnp.dot(n_ref[...], wv_ref[:, cols], preferred_element_type=f32).astype(
            bf16
        )
        return 0

    lax.fori_loop(0, D // 256, project, 0)

    lane = lax.broadcasted_iota(jnp.int32, (H, 128), 1)

    def slide(i, _):
        for a in [i * 4 + e for e in range(4)]:
            turn = jnp.bitwise_and(a + 1, 127)
            tiles = [pltpu.roll(rt_ref[:, 128 * j : 128 * (j + 1)], turn, 1) for j in range(9)]
            for j in range(8):
                s_ref[j, pl.ds(pl.multiple_of(a * H, H), H), :] = jnp.where(
                    lane < a + 1, tiles[j], tiles[j + 1]
                )
        return 0

    lax.fori_loop(0, TOK // 4, slide, 0)

    turned = s_ref.reshape(8, TOK, H, 128)
    wanted = b_ref.reshape(4, TOK, H, 128)

    def pick(i, _):
        for a in [i * 8 + e for e in range(8)]:
            for j in range(4):
                wanted[j, a] = turned[pos_ref[0, a] + j, pos_ref[1, a]]
        return 0

    lax.fori_loop(0, TOK // 8, pick, 0)

    row = lax.broadcasted_iota(jnp.int32, (TOK, KEYS), 0)
    col = lax.broadcasted_iota(jnp.int32, (TOK, KEYS), 1)
    mask_ref[...] = jnp.where(
        (col >= LMAX + row - place_ref[...]) & (col <= LMAX + row), 0.0, NEG
    )

    first = grp_ref[...] == 0
    first2 = jnp.concatenate([first, first], axis=0)
    half = lax.broadcasted_iota(jnp.int32, (TOK, 128), 1) < 64
    nt = (((1,), (1,)), ((), ()))

    def heads(p, _):
        cols = pl.ds(pl.multiple_of(p * 128, 128), 128)
        q = q_ref[:, cols].astype(f32)
        qq = jnp.concatenate([jnp.where(half, q, 0.0), jnp.where(half, 0.0, q)], axis=0)
        qg = jnp.concatenate(
            [jnp.where(first2, qq, 0.0), jnp.where(first2, 0.0, qq)], axis=1
        ).astype(bf16)
        kcat = jnp.concatenate(
            [pk_ref[:, s, :, cols].reshape(PREFIX, 128) for s in range(2)], axis=1
        )
        vcat = jnp.concatenate(
            [pv_ref[:, s, :, cols].reshape(PREFIX, 128) for s in range(2)], axis=1
        )
        def gather(ref, tiles):
            return jnp.concatenate(
                [
                    jnp.concatenate(
                        [ref[j, pl.ds(2 * p + e, TOK, stride=H), :] for j in tiles], axis=1
                    )
                    for e in range(2)
                ],
                axis=0,
            )

        mask = mask_ref[...]
        suf = (
            lax.dot_general(qq.astype(bf16), k_ref[:, cols], nt, preferred_element_type=f32)
            + gather(s_ref, range(3, 8))
            + jnp.concatenate([mask, mask], axis=0)
        )
        pre = lax.dot_general(qg, kcat, nt, preferred_element_type=f32) + gather(b_ref, range(4))
        top = jnp.maximum(
            jnp.max(suf, axis=1, keepdims=True), jnp.max(pre, axis=1, keepdims=True)
        )
        esuf = jnp.exp(suf - top)
        epre = jnp.exp(pre - top)
        total = jnp.sum(esuf, axis=1, keepdims=True) + jnp.sum(epre, axis=1, keepdims=True)
        osuf = jnp.dot(esuf.astype(bf16), v_ref[:, cols], preferred_element_type=f32)
        opre = jnp.dot(epre.astype(bf16), vcat, preferred_element_type=f32)
        o = (osuf + jnp.where(first2, opre[:, :128], opre[:, 128:])) / total
        mix_ref[:, cols] = jnp.where(half, o[:TOK], o[TOK:]).astype(bf16)
        return 0

    lax.fori_loop(0, H // 2, heads, 0)

    out_ref[...] = jnp.dot(mix_ref[...], wo_ref[...], preferred_element_type=f32).astype(bf16)


def layer(pos, slots, hid, pre, gain, rt, grp, place, wq, wk, wv, wo):
    vmem = pl.BlockSpec(memory_space=pltpu.VMEM)
    smem = pl.BlockSpec(memory_space=pltpu.SMEM)
    hbm = pl.BlockSpec(memory_space=pl.ANY)
    bf16 = jnp.bfloat16
    return pl.pallas_call(
        layer_kernel,
        out_shape=jax.ShapeDtypeStruct((TOK, D), bf16),
        in_specs=[smem] * 2 + [vmem] * 6 + [hbm] * 4,
        out_specs=vmem,
        scratch_shapes=[pltpu.VMEM((D, D), bf16)] * 4
        + [
            pltpu.VMEM((8, 8, 2 * D), bf16),
            pltpu.VMEM((4, 2, 8, 2 * D), bf16),
            pltpu.VMEM((KEYS, D), bf16),
            pltpu.VMEM((16, 2, 32, D), bf16),
            pltpu.VMEM((16, 2, 32, D), bf16),
            pltpu.VMEM((KEYS, D), bf16),
            pltpu.VMEM((TOK, D), bf16),
            pltpu.VMEM((KEYS, D), bf16),
            pltpu.VMEM((KEYS, D), bf16),
            pltpu.VMEM((8, TOK * H, 128), jnp.float32),
            pltpu.VMEM((4, TOK * H, 128), jnp.float32),
            pltpu.VMEM((TOK, KEYS), jnp.float32),
            pltpu.VMEM((TOK, D), bf16),
            pltpu.SemaphoreType.DMA((80,)),
            pltpu.SemaphoreType.DMA((80,)),
            pltpu.SemaphoreType.DMA((4,)),
        ],
        compiler_params=pltpu.CompilerParams(
            vmem_limit_bytes=58 << 20, collective_id=0, has_side_effects=True
        ),
        name="layer",
    )(pos, slots, hid, pre, gain, rt, grp, place, wq, wk, wv, wo)


def shards(
    hidden,
    ln_gain,
    w_query,
    w_key,
    w_value,
    w_out,
    rel_bias,
    prefix_cache,
    bucket_of_distance,
    slot_of_group,
    suffix_lengths,
    request_group,
):
    tp_index = lax.axis_index("tp")
    lens = suffix_lengths[0]
    ends = jnp.cumsum(lens)
    starts = ends - lens
    rows = tp_index * TOK + jnp.arange(TOK)
    req = jnp.minimum(jnp.sum((rows[:, None] >= ends[None, :]).astype(jnp.int32), axis=1), 127)
    onehot = req[:, None] == jnp.arange(lens.shape[0])[None, :]
    pos = rows - jnp.sum(jnp.where(onehot, starts[None, :], 0), axis=1)
    grp = jnp.sum(jnp.where(onehot, request_group[0][None, :], 0), axis=1)

    table = jnp.dot(
        rel_bias.T,
        jax.nn.one_hot(bucket_of_distance[::-1], rel_bias.shape[0], dtype=jnp.float32, axis=0),
        precision=lax.Precision.HIGHEST,
    )
    rt = jnp.pad(table, ((0, 0), (0, 128)))
    off = PREFIX - 1 - pos
    return layer(
        jnp.stack([off // 128, 127 - off % 128]),
        slot_of_group,
        hidden,
        prefix_cache.reshape(2, 8, 2 * D),
        ln_gain[None, :],
        rt,
        grp[:, None],
        pos[:, None],
        w_query,
        w_key,
        w_value,
        w_out,
    )


def solution(mesh):
    in_specs = (
        P(("grp", "tp"), None),
        P(),
        P(),
        P(),
        P(),
        P(),
        P(),
        P("grp", "tp", None, None),
        P(),
        P(),
        P("grp", None),
        P("grp", None),
    )
    out_specs = P(("grp", "tp"), None)
    return jax.shard_map(shards, mesh=mesh, in_specs=in_specs, out_specs=out_specs, check_vma=False)
```

```python
import jax
import jax.numpy as jnp
from jax import lax
from jax.experimental import pallas as pl
from jax.experimental.pallas import tpu as pltpu
from jax.sharding import PartitionSpec as P

D = 1024
H = 16
NB = 32
TOK = 128
LMAX = 512
KEYS = LMAX + TOK
PREFIX = 512
NEG = -1e30
MESH = pl.DeviceIdType.MESH
F32 = jnp.float32
BF16 = jnp.bfloat16
NT = (((1,), (1,)), ((), ()))


def iota(shape, dim):
    return lax.broadcasted_iota(jnp.int32, shape, dim)


def layer_kernel(
    slot_ref,
    hid_ref,
    pre_ref,
    gain_ref,
    bucket_ref,
    rel_ref,
    lens_ref,
    group_ref,
    wq_hbm,
    wk_hbm,
    wv_hbm,
    out_ref,
    wq_ref,
    wk_ref,
    wv_ref,
    own_ref,
    z_ref,
    all_ref,
    pk_ref,
    pv_ref,
    n_ref,
    q_ref,
    k_ref,
    v_ref,
    rt_ref,
    s_ref,
    b_ref,
    mask_ref,
    first_ref,
    o_ref,
    top_ref,
    sum_ref,
    at_ref,
    at_smem,
    send_sem,
    recv_sem,
    load_sem,
):
    g = lax.axis_index("grp")
    t = lax.axis_index("tp")
    y, x, z = t // 16, (t // 4) % 4, t % 4

    def tp_id(i):
        return (g, lax.rem(i + 128, 64))

    def z_id(d):
        return (g, y * 16 + x * 4 + lax.rem(z + d + 4, 4))

    def x_id(d):
        return (g, y * 16 + lax.rem(x + d + 4, 4) * 4 + z)

    def y_id(d):
        return (g, lax.rem(y + d + 4, 4) * 16 + x * 4 + z)

    used = []

    def copy(src, dst, device):
        i = len(used)
        out = pltpu.make_async_remote_copy(
            src_ref=src,
            dst_ref=dst,
            send_sem=send_sem.at[i],
            recv_sem=recv_sem.at[i],
            device_id=device,
            device_id_type=MESH,
        )
        out.start()
        used.append(out)
        return out

    row_ids = [(lax.rem(g + d, 4), t) for d in (1, 2, 3)]
    greet = row_ids + [tp_id(t + d) for d in (4, -4)]
    greet = greet + [ring(d) for ring in (x_id, y_id, z_id) for d in (1, -1)]
    barrier = pltpu.get_barrier_semaphore()
    for device in greet:
        pl.semaphore_signal(barrier, inc=1, device_id=device, device_id_type=MESH)

    loads = [
        pltpu.make_async_copy(src, dst, load_sem.at[i])
        for i, (src, dst) in enumerate([(wq_hbm, wq_ref), (wk_hbm, wk_ref), (wv_hbm, wv_ref)])
    ]
    for load in loads:
        load.start()

    def places():
        sub, lane = iota((TOK, TOK), 0), iota((TOK, TOK), 1)
        eye = sub == lane
        lens = jnp.sum(jnp.where(eye, lens_ref[...], 0).astype(F32), axis=1, keepdims=True)
        starts = jnp.sum(jnp.where(sub < lane, lens, 0.0), axis=0, keepdims=True)
        rows = (t * TOK + iota((TOK, 1), 0)).astype(F32)
        begun = starts <= rows
        place = rows - jnp.max(jnp.where(begun, starts, 0.0), axis=1, keepdims=True)
        req = jnp.sum(begun.astype(F32), axis=1, keepdims=True) - 1.0
        mine = lane.astype(F32) == req
        group = jnp.sum(
            jnp.where(mine, group_ref[...], 0).astype(F32), axis=1, keepdims=True
        )
        first_ref[...] = jnp.broadcast_to(group, (TOK, TOK))
        off = (PREFIX - 1) - jnp.sum(
            jnp.where(eye, place, 0.0), axis=0, keepdims=True
        ).astype(jnp.int32)
        off = jnp.clip(off, 0, PREFIX - 1)
        at_ref[...] = jnp.concatenate(
            [jnp.right_shift(off, 7), 127 - jnp.bitwise_and(off, 127)], axis=0
        )
        move = pltpu.make_async_copy(at_ref, at_smem, load_sem.at[3])
        move.start()
        row, col = iota((TOK, KEYS), 0), iota((TOK, KEYS), 1)
        low = LMAX + row - place.astype(jnp.int32)
        mask_ref[...] = jnp.where((col >= low) & (col <= LMAX + row), 0.0, NEG)
        move.wait()

    def table():
        flip = (iota((TOK, TOK), 0) + iota((TOK, TOK), 1) == TOK - 1).astype(BF16)
        bucket = jnp.dot(
            bucket_ref[...].astype(F32).astype(BF16), flip, preferred_element_type=F32
        ).astype(jnp.int32)
        for j in range(8):
            onehot = (iota((NB, 128), 0) == bucket[7 - j : 8 - j, :]).astype(F32)
            rt_ref[:, 128 * j : 128 * (j + 1)] = lax.dot_general(
                rel_ref[...],
                onehot,
                (((1,), (0,)), ((), ())),
                precision=lax.Precision.HIGHEST,
                preferred_element_type=F32,
            )
        rt_ref[:, 1024:] = jnp.zeros((H, 128), F32)

    def slides():
        lane = iota((H, 128), 1)

        def slide(i, _):
            for a in [i * 4 + e for e in range(4)]:
                turn = jnp.bitwise_and(a + 1, 127)
                tiles = [
                    pltpu.roll(rt_ref[:, 128 * j : 128 * (j + 1)], turn, 1) for j in range(9)
                ]
                for j in range(8):
                    s_ref[j, pl.ds(pl.multiple_of(a * H, H), H), :] = jnp.where(
                        lane < a + 1, tiles[j], tiles[j + 1]
                    )
            return 0

        lax.fori_loop(0, TOK // 4, slide, 0)

    def picks():
        turned = s_ref.reshape(8, TOK, H, 128)
        wanted = b_ref.reshape(4, TOK, H, 128)

        def pick(i, _):
            for a in [i * 8 + e for e in range(8)]:
                for j in range(4):
                    wanted[j, a] = turned[at_smem[0, a] + j, at_smem[1, a]]
            return 0

        lax.fori_loop(0, TOK // 8, pick, 0)

    gain = jnp.concatenate([gain_ref[j : j + 1, :].astype(F32) for j in range(8)], axis=1)

    def norms(i):
        h = all_ref[i].astype(F32)
        ms = jnp.mean(h * h, axis=1, keepdims=True)
        n_ref[i] = (h * lax.rsqrt(ms + 1e-06) * gain).astype(BF16)

    def projects(blocks, pairs):
        for w_ref, dst_ref in pairs:

            def project(i, _):
                cols = pl.ds(pl.multiple_of(i * 256, 256), 256)
                n = jnp.concatenate([n_ref[b] for b in blocks], axis=0)
                r = jnp.dot(n, w_ref[:, cols], preferred_element_type=F32).astype(BF16)
                for j, b in enumerate(blocks):
                    dst_ref[b, :, cols] = r[TOK * j : TOK * (j + 1)]
                return 0

            lax.fori_loop(0, D // 256, project, 0)

    half = iota((TOK, 128), 1) < 64

    def stacked(cols):
        q = q_ref[4, :, cols].astype(F32)
        return jnp.concatenate([jnp.where(half, q, 0.0), jnp.where(half, 0.0, q)], axis=0)

    def gather(ref, p, tiles):
        return jnp.concatenate(
            [
                jnp.concatenate(
                    [ref[j, pl.ds(2 * p + e, TOK, stride=H), :] for j in tiles], axis=1
                )
                for e in range(2)
            ],
            axis=0,
        )

    def suffix():
        def heads(p, _):
            cols = pl.ds(pl.multiple_of(p * 128, 128), 128)
            qq = stacked(cols).astype(BF16)
            mask = mask_ref[...]
            keys = k_ref[:, :, cols].reshape(KEYS, 128)
            values = v_ref[:, :, cols].reshape(KEYS, 128)
            scores = (
                lax.dot_general(qq, keys, NT, preferred_element_type=F32)
                + gather(s_ref, p, range(3, 8))
                + jnp.concatenate([mask, mask], axis=0)
            )
            top = jnp.max(scores, axis=1, keepdims=True)
            e = jnp.exp(scores - top)
            top_ref[p] = jnp.broadcast_to(top, (2 * TOK, 128))
            sum_ref[p] = jnp.broadcast_to(jnp.sum(e, axis=1, keepdims=True), (2 * TOK, 128))
            o_ref[p] = jnp.dot(e.astype(BF16), values, preferred_element_type=F32)
            return 0

        lax.fori_loop(0, H // 2, heads, 0)

    def prefix():
        first = first_ref[...] == 0.0
        first2 = jnp.concatenate([first, first], axis=0)

        def heads(p, _):
            cols = pl.ds(pl.multiple_of(p * 128, 128), 128)
            qq = stacked(cols)
            qg = jnp.concatenate(
                [jnp.where(first2, qq, 0.0), jnp.where(first2, 0.0, qq)], axis=1
            ).astype(BF16)
            keys, values = [
                jnp.concatenate(
                    [ref[:, s, :, cols].reshape(PREFIX, 128) for s in range(2)], axis=1
                )
                for ref in (pk_ref, pv_ref)
            ]
            scores = lax.dot_general(
                qg, keys, NT, preferred_element_type=F32
            ) + gather(b_ref, p, range(4))
            old = top_ref[p]
            top = jnp.maximum(old, jnp.max(scores, axis=1, keepdims=True))
            e = jnp.exp(scores - top[:, :1])
            scale = jnp.exp(old - top)
            total = sum_ref[p] * scale + jnp.sum(e, axis=1, keepdims=True)
            o = jnp.dot(e.astype(BF16), values, preferred_element_type=F32)
            o = jnp.where(first2, o[:, :128], o[:, 128:])
            o = (o_ref[p] * scale + o) / total
            out_ref[:, cols] = jnp.where(half, o[:TOK], o[TOK:]).astype(BF16)
            return 0

        lax.fori_loop(0, H // 2, heads, 0)

    all_ref[4] = hid_ref[...]
    own_ref[pl.ds(2 * g, 2)] = pre_ref[...]
    pl.semaphore_wait(barrier, len(greet))

    rows = [copy(pre_ref, own_ref.at[pl.ds(2 * g, 2)], device) for device in row_ids]
    back4 = copy(hid_ref, all_ref.at[0], tp_id(t + 4))
    table()
    for c in rows:
        c.wait_recv()
    for s in range(2):
        slot = jnp.full((8, 2, D), slot_ref[2 * g + s], jnp.int32)
        chosen = own_ref[0].astype(F32)
        for i in range(1, 8):
            chosen = jnp.where(slot == i, own_ref[i].astype(F32), chosen)
        z_ref[z, s] = jnp.concatenate([chosen[:, 0, :], chosen[:, 1, :]], axis=1).astype(BF16)

    def spread(buf, piece, me, ring):
        part = buf.at[piece(me)]
        return [copy(part, part, ring(1)), copy(part, part, ring(-1))]

    def onward(buf, piece, me, ring, first, step):
        first[0 if step == 1 else 1].wait_recv()
        part = buf.at[piece(lax.rem(me - step + 4, 4))]
        return copy(part, part, ring(step))

    zs = [spread(z_ref, lambda i, s=s: (i, s), z, z_id) for s in range(2)]
    slides()
    zfwd = [
        onward(z_ref, lambda i, s=s: (i, s), z, z_id, zs[s], 1 - 2 * s) for s in range(2)
    ]
    back4.wait_recv()
    up = copy(all_ref.at[4 - 4 * ((z + 1) // 4)], all_ref.at[3], z_id(1))
    down = copy(all_ref.at[4 * ((4 - z) // 4)], all_ref.at[1], z_id(-1))
    places()
    zs[0][1].wait_recv()
    zs[1][0].wait_recv()
    for c in zfwd:
        c.wait_recv()

    for s in range(2):
        for i in range(2):
            both = jnp.concatenate(
                [z_ref[2 * i, s].astype(F32), z_ref[2 * i + 1, s].astype(F32)], axis=0
            ).astype(BF16)
            pk_ref[y * 4 + x, s, 16 * i : 16 * (i + 1), :] = both[:, :D]
            pv_ref[y * 4 + x, s, 16 * i : 16 * (i + 1), :] = both[:, D:]

    def at_x(i, other, s):
        return (other * 4 + i, s)

    def at_y(i, other, s):
        return (i * 4 + other, s)

    lines = []
    for s in range(2):
        lines.append((pk_ref, s, x, y, x_id, y_id, at_x, at_y))
        lines.append((pv_ref, s, y, x, y_id, x_id, at_y, at_x))
    one = []
    for buf, s, me, other, ring, _, at, _ in lines:
        one.append(spread(buf, lambda i, s=s, at=at, o=other: at(i, o, s), me, ring))

    def second(line, shift):
        buf, s, me, other, _, ring, _, at = line
        chunk = lax.rem(me + shift + 4, 4)
        return spread(buf, lambda i: at(i, chunk, s), other, ring)

    def second_on(line, shift, first):
        buf, s, me, other, _, ring, _, at = line
        chunk = lax.rem(me + shift + 4, 4)
        step = 1 - 2 * s
        return onward(buf, lambda i: at(i, chunk, s), other, ring, first, step)

    two = [{0: second(line, 0)} for line in lines]
    norms(4)
    for load in loads:
        load.wait()
    projects((4,), [(wq_ref, q_ref), (wk_ref, k_ref), (wv_ref, v_ref)])
    far = []
    for line, first, rest in zip(lines, one, two):
        buf, s, me, other, ring, _, at, _ = line
        step = 1 - 2 * s
        far.append(onward(buf, lambda i: at(i, other, s), me, ring, first, step))
        rest[-step] = second(line, -step)
    for line, first, rest in zip(lines, one, two):
        step = 1 - 2 * line[1]
        first[1 if step == 1 else 0].wait_recv()
        rest[step] = second(line, step)

    picks()
    last = [second_on(line, 0, rest[0]) for line, rest in zip(lines, two)]
    for line, rest, c in zip(lines, two, far):
        c.wait_recv()
        rest[2] = second(line, 2)

    up.wait_recv()
    down.wait_recv()
    odd = lax.rem(z, 2)
    back2 = copy(all_ref.at[3 - 2 * odd], all_ref.at[2], z_id(1 - 2 * odd))
    for i in (0, 1, 3):
        norms(i)
    projects((0, 1, 3), [(wk_ref, k_ref), (wv_ref, v_ref)])
    for shift in (1, -1, 2):
        last = last + [
            second_on(line, shift, rest[shift]) for line, rest in zip(lines, two)
        ]
    back2.wait_recv()
    norms(2)
    projects((2,), [(wk_ref, k_ref), (wv_ref, v_ref)])
    suffix()
    for line, rest in zip(lines, two):
        step = 1 - 2 * line[1]
        for shift in (0, 1, -1, 2):
            rest[shift][1 if step == 1 else 0].wait_recv()
    for c in last:
        c.wait_recv()
    prefix()
    for c in used:
        c.wait_send()


def layer(slots, hid, pre, gain, bucket, rel, lens, group, wq, wk, wv):
    vmem = pl.BlockSpec(memory_space=pltpu.VMEM)
    smem = pl.BlockSpec(memory_space=pltpu.SMEM)
    hbm = pl.BlockSpec(memory_space=pl.ANY)
    pair = pltpu.VMEM((H // 2, 2 * TOK, 128), F32)
    return pl.pallas_call(
        layer_kernel,
        out_shape=jax.ShapeDtypeStruct((TOK, D), BF16),
        in_specs=[smem] + [vmem] * 7 + [hbm] * 3,
        out_specs=vmem,
        scratch_shapes=[pltpu.VMEM((D, D), BF16)] * 3
        + [
            pltpu.VMEM((8, 8, 2, D), BF16),
            pltpu.VMEM((4, 2, 8, 2 * D), BF16),
            pltpu.VMEM((5, TOK, D), BF16),
            pltpu.VMEM((16, 2, 32, D), BF16),
            pltpu.VMEM((16, 2, 32, D), BF16),
            pltpu.VMEM((5, TOK, D), BF16),
            pltpu.VMEM((5, TOK, D), BF16),
            pltpu.VMEM((5, TOK, D), BF16),
            pltpu.VMEM((5, TOK, D), BF16),
            pltpu.VMEM((H, 1152), F32),
            pltpu.VMEM((8, TOK * H, 128), F32),
            pltpu.VMEM((4, TOK * H, 128), F32),
            pltpu.VMEM((TOK, KEYS), F32),
            pltpu.VMEM((TOK, TOK), F32),
            pair,
            pair,
            pair,
            pltpu.VMEM((2, TOK), jnp.int32),
            pltpu.SMEM((2, TOK), jnp.int32),
            pltpu.SemaphoreType.DMA((80,)),
            pltpu.SemaphoreType.DMA((80,)),
            pltpu.SemaphoreType.DMA((4,)),
        ],
        compiler_params=pltpu.CompilerParams(
            vmem_limit_bytes=58 << 20, collective_id=0, has_side_effects=True
        ),
        name="layer",
    )(slots, hid, pre, gain, bucket, rel, lens, group, wq, wk, wv)


def shards(
    hidden,
    ln_gain,
    w_query,
    w_key,
    w_value,
    w_out,
    rel_bias,
    prefix_cache,
    bucket_of_distance,
    slot_of_group,
    suffix_lengths,
    request_group,
):
    mixed = layer(
        slot_of_group,
        hidden,
        prefix_cache,
        ln_gain.reshape(8, 128),
        bucket_of_distance.reshape(8, 128),
        rel_bias.T,
        suffix_lengths,
        request_group,
        w_query,
        w_key,
        w_value,
    )
    return jnp.dot(mixed, w_out, preferred_element_type=jnp.float32).astype(jnp.bfloat16)


def solution(mesh):
    in_specs = (
        P(("grp", "tp"), None),
        P(),
        P(),
        P(),
        P(),
        P(),
        P(),
        P("grp", "tp", None, None),
        P(),
        P(),
        P("grp", None),
        P("grp", None),
    )
    out_specs = P(("grp", "tp"), None)
    return jax.shard_map(shards, mesh=mesh, in_specs=in_specs, out_specs=out_specs, check_vma=False)
```

```python
import jax
import jax.numpy as jnp
from jax import lax
from jax.experimental import pallas as pl
from jax.experimental.pallas import tpu as pltpu
from jax.sharding import PartitionSpec as P

D = 1024
H = 16
NB = 32
TOK = 128
LMAX = 512
KEYS = LMAX + TOK
PREFIX = 512
NEG = -1e30
MESH = pl.DeviceIdType.MESH
F32 = jnp.float32
BF16 = jnp.bfloat16
UNROLL = 4
NT = (((1,), (1,)), ((), ()))


def iota(shape, dim):
    return lax.broadcasted_iota(jnp.int32, shape, dim)


def layer_kernel(
    slot_ref,
    hid_ref,
    pre_ref,
    gain_ref,
    bucket_ref,
    rel_ref,
    lens_ref,
    group_ref,
    wq_hbm,
    wk_hbm,
    wv_hbm,
    out_ref,
    wq_ref,
    wk_ref,
    wv_ref,
    own_ref,
    z_ref,
    all_ref,
    pk_ref,
    pv_ref,
    n_ref,
    q_ref,
    k_ref,
    v_ref,
    rt_ref,
    s_ref,
    b_ref,
    mask_ref,
    first_ref,
    o_ref,
    top_ref,
    sum_ref,
    at_ref,
    at_smem,
    send_sem,
    recv_sem,
    load_sem,
):
    g = lax.axis_index("grp")
    t = lax.axis_index("tp")
    y, x, z = t // 16, (t // 4) % 4, t % 4

    def tp_id(i):
        return (g, lax.rem(i + 128, 64))

    def z_id(d):
        return (g, y * 16 + x * 4 + lax.rem(z + d + 4, 4))

    def x_id(d):
        return (g, y * 16 + lax.rem(x + d + 4, 4) * 4 + z)

    def y_id(d):
        return (g, lax.rem(y + d + 4, 4) * 16 + x * 4 + z)

    used = []

    def copy(src, dst, device):
        i = len(used)
        out = pltpu.make_async_remote_copy(
            src_ref=src,
            dst_ref=dst,
            send_sem=send_sem.at[i],
            recv_sem=recv_sem.at[i],
            device_id=device,
            device_id_type=MESH,
        )
        out.start()
        used.append(out)
        return out

    row_ids = [(lax.rem(g + d, 4), t) for d in (1, 2, 3)]
    greet = row_ids + [tp_id(t + d) for d in (4, -4)]
    greet = greet + [ring(d) for ring in (x_id, y_id, z_id) for d in (1, -1)]
    barrier = pltpu.get_barrier_semaphore()
    for device in greet:
        pl.semaphore_signal(barrier, inc=1, device_id=device, device_id_type=MESH)

    loads = [
        pltpu.make_async_copy(src, dst, load_sem.at[i])
        for i, (src, dst) in enumerate([(wq_hbm, wq_ref), (wk_hbm, wk_ref), (wv_hbm, wv_ref)])
    ]
    for load in loads:
        load.start()

    def places():
        sub, lane = iota((TOK, TOK), 0), iota((TOK, TOK), 1)
        eye = sub == lane
        lens = jnp.sum(jnp.where(eye, lens_ref[...], 0).astype(F32), axis=1, keepdims=True)
        starts = jnp.sum(jnp.where(sub < lane, lens, 0.0), axis=0, keepdims=True)
        rows = (t * TOK + iota((TOK, 1), 0)).astype(F32)
        begun = starts <= rows
        place = rows - jnp.max(jnp.where(begun, starts, 0.0), axis=1, keepdims=True)
        req = jnp.sum(begun.astype(F32), axis=1, keepdims=True) - 1.0
        mine = lane.astype(F32) == req
        group = jnp.sum(
            jnp.where(mine, group_ref[...], 0).astype(F32), axis=1, keepdims=True
        )
        first_ref[...] = jnp.broadcast_to(group, (TOK, TOK))
        off = (PREFIX - 1) - jnp.sum(
            jnp.where(eye, place, 0.0), axis=0, keepdims=True
        ).astype(jnp.int32)
        off = jnp.clip(off, 0, PREFIX - 1)
        at_ref[...] = jnp.concatenate(
            [jnp.right_shift(off, 7), 127 - jnp.bitwise_and(off, 127)], axis=0
        )
        move = pltpu.make_async_copy(at_ref, at_smem, load_sem.at[3])
        move.start()
        row, col = iota((TOK, 128), 0), iota((TOK, 128), 1)
        low = LMAX + row - place.astype(jnp.int32)
        for j in range(5):
            at = col + 128 * j
            mask_ref[j] = jnp.where((at >= low) & (at <= LMAX + row), 0.0, NEG)
        move.wait()

    def table():
        flip = (iota((TOK, TOK), 0) + iota((TOK, TOK), 1) == TOK - 1).astype(BF16)
        bucket = jnp.dot(
            bucket_ref[...].astype(F32).astype(BF16), flip, preferred_element_type=F32
        ).astype(jnp.int32)
        for j in range(8):
            onehot = (iota((NB, 128), 0) == bucket[7 - j : 8 - j, :]).astype(F32)
            rt_ref[:, 128 * j : 128 * (j + 1)] = lax.dot_general(
                rel_ref[...],
                onehot,
                (((1,), (0,)), ((), ())),
                precision=lax.Precision.HIGHEST,
                preferred_element_type=F32,
            )
        rt_ref[:, 1024:] = jnp.zeros((H, 128), F32)

    def slides(start, stop):
        lane = iota((H, 128), 1)

        def slide(i, _):
            for a in [i * 4 + e for e in range(4)]:
                turn = jnp.bitwise_and(a + 1, 127)
                tiles = [
                    pltpu.roll(rt_ref[:, 128 * j : 128 * (j + 1)], turn, 1) for j in range(9)
                ]
                for j in range(8):
                    s_ref[j, pl.ds(pl.multiple_of(a * H, H), H), :] = jnp.where(
                        lane < a + 1, tiles[j], tiles[j + 1]
                    )
            return 0

        lax.fori_loop(start // 4, stop // 4, slide, 0)

    def picks():
        turned = s_ref.reshape(8, TOK, H, 128)
        wanted = b_ref.reshape(4, TOK, H, 128)

        def pick(i, _):
            for a in [i * 8 + e for e in range(8)]:
                for j in range(4):
                    wanted[j, a] = turned[at_smem[0, a] + j, at_smem[1, a]]
            return 0

        lax.fori_loop(0, TOK // 8, pick, 0)

    gain = jnp.concatenate([gain_ref[j : j + 1, :].astype(F32) for j in range(8)], axis=1)

    def norms(i):
        h = all_ref[i].astype(F32)
        ms = jnp.mean(h * h, axis=1, keepdims=True)
        n_ref[i] = (h * lax.rsqrt(ms + 1e-06) * gain).astype(BF16)

    def projects(blocks, pairs):
        for w_ref, dst_ref in pairs:

            def project(i, _):
                cols = pl.ds(pl.multiple_of(i * 256, 256), 256)
                n = jnp.concatenate([n_ref[b] for b in blocks], axis=0)
                r = jnp.dot(n, w_ref[:, cols], preferred_element_type=F32).astype(BF16)
                for j, b in enumerate(blocks):
                    dst_ref[b, :, cols] = r[TOK * j : TOK * (j + 1)]
                return 0

            lax.fori_loop(0, D // 256, project, 0)

    half = iota((TOK, 128), 1) < 64

    def stacked(cols):
        q = q_ref[4, :, cols].astype(F32)
        return jnp.concatenate([jnp.where(half, q, 0.0), jnp.where(half, 0.0, q)], axis=0)

    def gather(ref, p, tiles):
        return jnp.concatenate(
            [
                jnp.concatenate(
                    [ref[j, pl.ds(2 * p + e, TOK, stride=H), :] for j in tiles], axis=1
                )
                for e in range(2)
            ],
            axis=0,
        )

    def update(p, sets, begin, end):
        wide = (2 * TOK, 128)
        tops = [jnp.max(scores, axis=1, keepdims=True) for scores, _, _ in sets]
        top = jnp.broadcast_to(tops[0] if len(tops) == 1 else jnp.maximum(*tops), wide)
        if not begin:
            old = top_ref[p]
            top = jnp.maximum(old, top)
            scale = jnp.exp(old - top)
        total, o = 0.0, 0.0
        for scores, values, first2 in sets:
            e = jnp.exp(scores - jnp.concatenate([top] * (scores.shape[1] // 128), axis=1))
            total = total + jnp.broadcast_to(jnp.sum(e, axis=1, keepdims=True), wide)
            part = jnp.dot(e.astype(BF16), values, preferred_element_type=F32)
            if first2 is not None:
                part = jnp.where(first2, part[:, :128], part[:, 128:])
            o = o + part
        if not begin:
            total = sum_ref[p] * scale + total
            o = o_ref[p] * scale + o
        if end:
            o = o / total
            cols = pl.ds(pl.multiple_of(p * 128, 128), 128)
            out_ref[:, cols] = jnp.where(half, o[:TOK], o[TOK:]).astype(BF16)
        else:
            top_ref[p] = top
            sum_ref[p] = total
            o_ref[p] = o

    def suffix_set(p, blocks):
        cols = pl.ds(pl.multiple_of(p * 128, 128), 128)
        keys, values = [
            jnp.concatenate([ref[b, :, cols] for b in blocks], axis=0) for ref in (k_ref, v_ref)
        ]
        mask = jnp.concatenate([mask_ref[b] for b in blocks], axis=1)
        scores = (
            lax.dot_general(stacked(cols).astype(BF16), keys, NT, preferred_element_type=F32)
            + gather(s_ref, p, [b + 3 for b in blocks])
            + jnp.concatenate([mask, mask], axis=0)
        )
        return scores, values, None

    def prefix_set(p, h, i, first2):
        part = pl.ds(pl.multiple_of(i * 128, 128), 128)
        qq = stacked(pl.ds(pl.multiple_of(p * 128, 128), 128))
        qg = jnp.concatenate(
            [jnp.where(first2, qq, 0.0), jnp.where(first2, 0.0, qq)], axis=1
        ).astype(BF16)
        keys, values = [
            jnp.concatenate(
                [ref[h, :, s, :, part].reshape(PREFIX, 128) for s in range(2)], axis=1
            )
            for ref in (pk_ref, pv_ref)
        ]
        scores = lax.dot_general(qg, keys, NT, preferred_element_type=F32)
        return scores + gather(b_ref, p, range(4)), values, first2

    def suffix(blocks, start, stop, begin, end):
        def heads(p, _):
            update(p, [suffix_set(p, blocks)], begin, end)
            return 0

        lax.fori_loop(start, stop, heads, 0, unroll=UNROLL)

    def prefix(h, blocks, end):
        def heads(i, _):
            first = first_ref[...] == 0.0
            first2 = jnp.concatenate([first, first], axis=0)
            p = 4 * h + i
            sets = [prefix_set(p, h, i, first2)]
            if blocks:
                sets.append(suffix_set(p, blocks))
            update(p, sets, False, end)
            return 0

        lax.fori_loop(0, 4, heads, 0, unroll=UNROLL)

    all_ref[4] = hid_ref[...]
    mine = pl.ds(2 * g, 2)
    for i in range(2):
        raw = pre_ref[i].astype(F32)
        own_ref[2 * g + i] = jnp.concatenate([raw[:, 0, :], raw[:, 1, :]], axis=1).astype(BF16)
    table()
    places()
    pl.semaphore_wait(barrier, len(greet))

    rows = [copy(own_ref.at[mine], own_ref.at[mine], device) for device in row_ids]
    back4 = copy(hid_ref, all_ref.at[0], tp_id(t + 4))
    slides(0, TOK // 2)
    for c in rows:
        c.wait_recv()
    for i in range(2):
        z_ref[z, i] = own_ref[slot_ref[2 * g + i]]

    def spread(part, ring):
        return [copy(part, part, ring(1)), copy(part, part, ring(-1))]

    def onward(part, me, ring, first):
        out = []
        for i, step in ((0, 1), (1, -1)):
            first[i].wait_recv()
            piece = part(lax.rem(me - step + 4, 4)).at[i]
            out.append(copy(piece, piece, ring(step)))
        return out

    own = z_ref.at[z]
    ahead = [copy(own.at[i], own.at[i], z_id(1 - 2 * i)) for i in range(2)]
    rest = [copy(own.at[i], own.at[i], z_id(2 * i - 1)) for i in range(2)]
    slides(TOK // 2, TOK)
    zfwd = onward(lambda i: z_ref.at[i], z, z_id, ahead)
    norms(4)
    for load in loads:
        load.wait()
    projects((4,), [(wq_ref, q_ref), (wk_ref, k_ref), (wv_ref, v_ref)])
    for c in rest + zfwd:
        c.wait_recv()

    def place_own(h):
        for i in range(2):
            for j in range(2):
                both = jnp.concatenate(
                    [z_ref[2 * j, i].astype(F32), z_ref[2 * j + 1, i].astype(F32)], axis=0
                ).astype(BF16)
                low = D // 2 * h
                rows = slice(16 * j, 16 * (j + 1))
                pk_ref[h, y * 4 + x, i, rows, :] = both[:, low : low + D // 2]
                pv_ref[h, y * 4 + x, i, rows, :] = both[:, D + low : D + low + D // 2]

    def line(h, swap):
        buf = (pv_ref if swap else pk_ref).at[h]
        me, other = (y, x) if swap else (x, y)
        ring, ring2 = (y_id, x_id) if swap else (x_id, y_id)

        def at(i, j):
            return buf.at[i * 4 + j] if swap else buf.at[j * 4 + i]

        state = {}

        def start():
            state["one"] = spread(at(me, other), ring)
            state[0] = spread(at(me, other), ring2)

        def second(shift):
            state[shift] = spread(at(lax.rem(me + shift + 4, 4), other), ring2)

        def turn():
            state["far"] = onward(lambda i: at(i, other), me, ring, state["one"])
            second(-1)
            second(1)

        def last():
            for c in state["far"]:
                c.wait_recv()
            second(2)

        def on(shift):
            state[shift, 2] = onward(
                lambda j: at(lax.rem(me + shift + 4, 4), j), other, ring2, state[shift]
            )

        def done():
            for shift in (0, -1, 1, 2):
                for c in state[shift, 2]:
                    c.wait_recv()

        return dict(start=start, turn=turn, last=last, on=on, done=done)

    lines = [[line(h, False), line(h, True)] for h in range(2)]

    def run(h, name, *args):
        for item in lines[h]:
            item[name](*args)

    for h in range(2):
        place_own(h)
        run(h, "start")
    back4.wait_recv()
    from_up, from_down = 4 - 4 * ((z + 1) // 4), 4 * ((4 - z) // 4)
    odd = lax.rem(z, 2)
    parts = [pl.ds(TOK // 2 * i, TOK // 2) for i in range(2)]
    near = [
        [
            copy(all_ref.at[from_up, part], all_ref.at[3, part], z_id(1)),
            copy(all_ref.at[from_down, part], all_ref.at[1, part], z_id(-1)),
        ]
        for part in parts
    ]

    def two_back(i):
        for c in near[i]:
            c.wait_recv()
        return copy(
            all_ref.at[3 - 2 * odd, parts[i]], all_ref.at[2, parts[i]], z_id(1 - 2 * odd)
        )

    picks()
    run(0, "turn")
    run(1, "turn")
    norms(0)
    run(0, "on", 0)
    run(0, "last")
    back2 = [two_back(0)]
    run(1, "on", 0)
    run(1, "last")
    back2.append(two_back(1))
    norms(1)
    norms(3)
    projects((0, 1, 3), [(wk_ref, k_ref), (wv_ref, v_ref)])
    run(0, "on", -1)
    run(0, "on", 1)
    suffix((0, 1, 3, 4), 0, 4, True, False)
    run(1, "on", -1)
    run(1, "on", 1)
    run(0, "on", 2)
    suffix((0, 1, 3, 4), 4, 8, True, False)
    run(1, "on", 2)
    run(0, "done")
    prefix(0, (), False)
    for c in back2:
        c.wait_recv()
    norms(2)
    projects((2,), [(wk_ref, k_ref), (wv_ref, v_ref)])
    suffix((2,), 0, 4, False, True)
    run(1, "done")
    prefix(1, (2,), True)
    for c in used:
        c.wait_send()


def layer(slots, hid, pre, gain, bucket, rel, lens, group, wq, wk, wv):
    vmem = pl.BlockSpec(memory_space=pltpu.VMEM)
    smem = pl.BlockSpec(memory_space=pltpu.SMEM)
    hbm = pl.BlockSpec(memory_space=pl.ANY)
    pair = pltpu.VMEM((H // 2, 2 * TOK, 128), F32)
    return pl.pallas_call(
        layer_kernel,
        out_shape=jax.ShapeDtypeStruct((TOK, D), BF16),
        in_specs=[smem] + [vmem] * 7 + [hbm] * 3,
        out_specs=vmem,
        scratch_shapes=[pltpu.VMEM((D, D), BF16)] * 3
        + [
            pltpu.VMEM((8, 8, 2 * D), BF16),
            pltpu.VMEM((4, 2, 8, 2 * D), BF16),
            pltpu.VMEM((5, TOK, D), BF16),
            pltpu.VMEM((2, 16, 2, 32, D // 2), BF16),
            pltpu.VMEM((2, 16, 2, 32, D // 2), BF16),
            pltpu.VMEM((5, TOK, D), BF16),
            pltpu.VMEM((5, TOK, D), BF16),
            pltpu.VMEM((5, TOK, D), BF16),
            pltpu.VMEM((5, TOK, D), BF16),
            pltpu.VMEM((H, 1152), F32),
            pltpu.VMEM((8, TOK * H, 128), F32),
            pltpu.VMEM((4, TOK * H, 128), F32),
            pltpu.VMEM((5, TOK, 128), F32),
            pltpu.VMEM((TOK, TOK), F32),
            pair,
            pair,
            pair,
            pltpu.VMEM((2, TOK), jnp.int32),
            pltpu.SMEM((2, TOK), jnp.int32),
            pltpu.SemaphoreType.DMA((104,)),
            pltpu.SemaphoreType.DMA((104,)),
            pltpu.SemaphoreType.DMA((4,)),
        ],
        compiler_params=pltpu.CompilerParams(
            vmem_limit_bytes=58 << 20, collective_id=0, has_side_effects=True
        ),
        name="layer",
    )(slots, hid, pre, gain, bucket, rel, lens, group, wq, wk, wv)


def shards(
    hidden,
    ln_gain,
    w_query,
    w_key,
    w_value,
    w_out,
    rel_bias,
    prefix_cache,
    bucket_of_distance,
    slot_of_group,
    suffix_lengths,
    request_group,
):
    mixed = layer(
        slot_of_group,
        hidden,
        prefix_cache,
        ln_gain.reshape(8, 128),
        bucket_of_distance.reshape(8, 128),
        rel_bias.T,
        suffix_lengths,
        request_group,
        w_query,
        w_key,
        w_value,
    )
    return jnp.dot(mixed, w_out, preferred_element_type=jnp.float32).astype(jnp.bfloat16)


def solution(mesh):
    in_specs = (
        P(("grp", "tp"), None),
        P(),
        P(),
        P(),
        P(),
        P(),
        P(),
        P("grp", "tp", None, None),
        P(),
        P(),
        P("grp", None),
        P("grp", None),
    )
    out_specs = P(("grp", "tp"), None)
    return jax.shard_map(shards, mesh=mesh, in_specs=in_specs, out_specs=out_specs, check_vma=False)
```

```python
import jax
import jax.numpy as jnp
from jax import lax
from jax.experimental import pallas as pl
from jax.experimental.pallas import tpu as pltpu
from jax.sharding import PartitionSpec as P

D = 1024
H = 16
NB = 32
TOK = 128
LMAX = 512
KEYS = LMAX + TOK
PREFIX = 512
NEG = -1e30
MESH = pl.DeviceIdType.MESH
F32 = jnp.float32
BF16 = jnp.bfloat16
UNROLL = 4
NT = (((1,), (1,)), ((), ()))


def iota(shape, dim):
    return lax.broadcasted_iota(jnp.int32, shape, dim)


def layer_kernel(
    slot_ref,
    hid_ref,
    pre_ref,
    gain_ref,
    bucket_ref,
    rel_ref,
    lens_ref,
    group_ref,
    wq_hbm,
    wk_hbm,
    wv_hbm,
    out_ref,
    wq_ref,
    wk_ref,
    wv_ref,
    own_ref,
    z_ref,
    all_ref,
    pk_ref,
    pv_ref,
    n_ref,
    q_ref,
    k_ref,
    v_ref,
    rt_ref,
    s_ref,
    b_ref,
    mask_ref,
    first_ref,
    o_ref,
    top_ref,
    sum_ref,
    at_ref,
    at_smem,
    send_sem,
    recv_sem,
    load_sem,
):
    g = lax.axis_index("grp")
    t = lax.axis_index("tp")
    y, x, z = t // 16, (t // 4) % 4, t % 4

    def tp_id(i):
        return (g, lax.rem(i + 128, 64))

    def z_id(d):
        return (g, y * 16 + x * 4 + lax.rem(z + d + 4, 4))

    def x_id(d):
        return (g, y * 16 + lax.rem(x + d + 4, 4) * 4 + z)

    def y_id(d):
        return (g, lax.rem(y + d + 4, 4) * 16 + x * 4 + z)

    used = []

    def copy(src, dst, device):
        i = len(used)
        out = pltpu.make_async_remote_copy(
            src_ref=src,
            dst_ref=dst,
            send_sem=send_sem.at[i],
            recv_sem=recv_sem.at[i],
            device_id=device,
            device_id_type=MESH,
        )
        out.start()
        used.append(out)
        return out

    row_ids = [(lax.rem(g + d, 4), t) for d in (1, 2, 3)]
    greet = row_ids + [tp_id(t + d) for d in (4, -4)]
    greet = greet + [ring(d) for ring in (x_id, y_id, z_id) for d in (1, -1)]
    barrier = pltpu.get_barrier_semaphore()
    for device in greet:
        pl.semaphore_signal(barrier, inc=1, device_id=device, device_id_type=MESH)

    loads = [
        pltpu.make_async_copy(src, dst, load_sem.at[i])
        for i, (src, dst) in enumerate([(wq_hbm, wq_ref), (wk_hbm, wk_ref), (wv_hbm, wv_ref)])
    ]
    for load in loads:
        load.start()

    def places():
        sub, lane = iota((TOK, TOK), 0), iota((TOK, TOK), 1)
        eye = sub == lane
        lens = jnp.sum(jnp.where(eye, lens_ref[...], 0).astype(F32), axis=1, keepdims=True)
        starts = jnp.sum(jnp.where(sub < lane, lens, 0.0), axis=0, keepdims=True)
        rows = (t * TOK + iota((TOK, 1), 0)).astype(F32)
        begun = starts <= rows
        place = rows - jnp.max(jnp.where(begun, starts, 0.0), axis=1, keepdims=True)
        req = jnp.sum(begun.astype(F32), axis=1, keepdims=True) - 1.0
        mine = lane.astype(F32) == req
        group = jnp.sum(
            jnp.where(mine, group_ref[...], 0).astype(F32), axis=1, keepdims=True
        )
        first_ref[...] = jnp.broadcast_to(group, (TOK, TOK))
        off = (PREFIX - 1) - jnp.sum(
            jnp.where(eye, place, 0.0), axis=0, keepdims=True
        ).astype(jnp.int32)
        off = jnp.clip(off, 0, PREFIX - 1)
        at_ref[...] = jnp.concatenate(
            [jnp.right_shift(off, 7), 127 - jnp.bitwise_and(off, 127)], axis=0
        )
        move = pltpu.make_async_copy(at_ref, at_smem, load_sem.at[3])
        move.start()
        row, col = iota((TOK, 128), 0), iota((TOK, 128), 1)
        low = LMAX + row - place.astype(jnp.int32)
        for j in range(5):
            at = col + 128 * j
            mask_ref[j] = jnp.where((at >= low) & (at <= LMAX + row), 0.0, NEG)
        move.wait()

    def table():
        flip = (iota((TOK, TOK), 0) + iota((TOK, TOK), 1) == TOK - 1).astype(BF16)
        bucket = jnp.dot(
            bucket_ref[...].astype(F32).astype(BF16), flip, preferred_element_type=F32
        ).astype(jnp.int32)
        for j in range(8):
            onehot = (iota((NB, 128), 0) == bucket[7 - j : 8 - j, :]).astype(F32)
            rt_ref[:, 128 * j : 128 * (j + 1)] = lax.dot_general(
                rel_ref[...],
                onehot,
                (((1,), (0,)), ((), ())),
                precision=lax.Precision.HIGHEST,
                preferred_element_type=F32,
            )
        rt_ref[:, 1024:] = jnp.zeros((H, 128), F32)

    def slides(start, stop):
        lane = iota((H, 128), 1)

        def slide(i, _):
            for a in [i * 4 + e for e in range(4)]:
                turn = jnp.bitwise_and(a + 1, 127)
                tiles = [
                    pltpu.roll(rt_ref[:, 128 * j : 128 * (j + 1)], turn, 1) for j in range(9)
                ]
                for j in range(8):
                    s_ref[j, pl.ds(pl.multiple_of(a * H, H), H), :] = jnp.where(
                        lane < a + 1, tiles[j], tiles[j + 1]
                    )
            return 0

        lax.fori_loop(start // 4, stop // 4, slide, 0)

    def picks():
        turned = s_ref.reshape(8, TOK, H, 128)
        wanted = b_ref.reshape(4, TOK, H, 128)

        def pick(i, _):
            for a in [i * 8 + e for e in range(8)]:
                for j in range(4):
                    wanted[j, a] = turned[at_smem[0, a] + j, at_smem[1, a]]
            return 0

        lax.fori_loop(0, TOK // 8, pick, 0)

    gain = jnp.concatenate([gain_ref[j : j + 1, :].astype(F32) for j in range(8)], axis=1)

    def norms(i):
        h = all_ref[i].astype(F32)
        ms = jnp.mean(h * h, axis=1, keepdims=True)
        n_ref[i] = (h * lax.rsqrt(ms + 1e-06) * gain).astype(BF16)

    def projects(blocks, pairs):
        for w_ref, dst_ref in pairs:

            def project(i, _):
                cols = pl.ds(pl.multiple_of(i * 256, 256), 256)
                n = jnp.concatenate([n_ref[b] for b in blocks], axis=0)
                r = jnp.dot(n, w_ref[:, cols], preferred_element_type=F32).astype(BF16)
                for j, b in enumerate(blocks):
                    dst_ref[b, :, cols] = r[TOK * j : TOK * (j + 1)]
                return 0

            lax.fori_loop(0, D // 256, project, 0, unroll=UNROLL)

    half = iota((TOK, 128), 1) < 64

    def stacked(cols):
        q = q_ref[4, :, cols].astype(F32)
        return jnp.concatenate([jnp.where(half, q, 0.0), jnp.where(half, 0.0, q)], axis=0)

    def gather(ref, p, tiles):
        return jnp.concatenate(
            [
                jnp.concatenate(
                    [ref[j, pl.ds(2 * p + e, TOK, stride=H), :] for j in tiles], axis=1
                )
                for e in range(2)
            ],
            axis=0,
        )

    def update(p, sets, begin, end):
        wide = (2 * TOK, 128)
        tops = [jnp.max(scores, axis=1, keepdims=True) for scores, _, _ in sets]
        top = jnp.broadcast_to(tops[0] if len(tops) == 1 else jnp.maximum(*tops), wide)
        if not begin:
            old = top_ref[p]
            top = jnp.maximum(old, top)
            scale = jnp.exp(old - top)
        total, o = 0.0, 0.0
        for scores, values, first2 in sets:
            e = jnp.exp(scores - jnp.concatenate([top] * (scores.shape[1] // 128), axis=1))
            total = total + jnp.broadcast_to(jnp.sum(e, axis=1, keepdims=True), wide)
            part = jnp.dot(e.astype(BF16), values, preferred_element_type=F32)
            if first2 is not None:
                part = jnp.where(first2, part[:, :128], part[:, 128:])
            o = o + part
        if not begin:
            total = sum_ref[p] * scale + total
            o = o_ref[p] * scale + o
        if end:
            o = o / total
            cols = pl.ds(pl.multiple_of(p * 128, 128), 128)
            out_ref[:, cols] = jnp.where(half, o[:TOK], o[TOK:]).astype(BF16)
        else:
            top_ref[p] = top
            sum_ref[p] = total
            o_ref[p] = o

    def suffix_set(p, blocks):
        cols = pl.ds(pl.multiple_of(p * 128, 128), 128)
        keys, values = [
            jnp.concatenate([ref[b, :, cols] for b in blocks], axis=0) for ref in (k_ref, v_ref)
        ]
        mask = jnp.concatenate([mask_ref[b] for b in blocks], axis=1)
        scores = (
            lax.dot_general(stacked(cols).astype(BF16), keys, NT, preferred_element_type=F32)
            + gather(s_ref, p, [b + 3 for b in blocks])
            + jnp.concatenate([mask, mask], axis=0)
        )
        return scores, values, None

    def prefix_set(p, h, i, first2):
        part = pl.ds(pl.multiple_of(i * 128, 128), 128)
        qq = stacked(pl.ds(pl.multiple_of(p * 128, 128), 128))
        qg = jnp.concatenate(
            [jnp.where(first2, qq, 0.0), jnp.where(first2, 0.0, qq)], axis=1
        ).astype(BF16)
        keys, values = [
            jnp.concatenate(
                [ref[h, :, s, :, part].reshape(PREFIX, 128) for s in range(2)], axis=1
            )
            for ref in (pk_ref, pv_ref)
        ]
        scores = lax.dot_general(qg, keys, NT, preferred_element_type=F32)
        return scores + gather(b_ref, p, range(4)), values, first2

    def suffix(blocks, start, stop, begin, end):
        def heads(p, _):
            update(p, [suffix_set(p, blocks)], begin, end)
            return 0

        lax.fori_loop(start, stop, heads, 0, unroll=UNROLL)

    def prefix(h, blocks, end):
        def heads(i, _):
            first = first_ref[...] == 0.0
            first2 = jnp.concatenate([first, first], axis=0)
            p = 4 * h + i
            sets = [prefix_set(p, h, i, first2)]
            if blocks:
                sets.append(suffix_set(p, blocks))
            update(p, sets, False, end)
            return 0

        lax.fori_loop(0, 4, heads, 0, unroll=UNROLL)

    all_ref[4] = hid_ref[...]
    mine = pl.ds(2 * g, 2)
    for i in range(2):
        raw = pre_ref[i].astype(F32)
        own_ref[2 * g + i] = jnp.concatenate([raw[:, 0, :], raw[:, 1, :]], axis=1).astype(BF16)
    pl.semaphore_wait(barrier, len(greet))

    rows = [copy(own_ref.at[mine], own_ref.at[mine], device) for device in row_ids]
    back4 = copy(hid_ref, all_ref.at[0], tp_id(t + 4))
    table()
    slides(0, TOK // 2)
    for c in rows:
        c.wait_recv()
    for i in range(2):
        z_ref[z, i] = own_ref[slot_ref[2 * g + i]]

    def spread(part, ring):
        return [copy(part, part, ring(1)), copy(part, part, ring(-1))]

    def onward(part, me, ring, first):
        out = []
        for i, step in ((0, 1), (1, -1)):
            first[i].wait_recv()
            piece = part(lax.rem(me - step + 4, 4)).at[i]
            out.append(copy(piece, piece, ring(step)))
        return out

    own = z_ref.at[z]
    ahead = [copy(own.at[i], own.at[i], z_id(1 - 2 * i)) for i in range(2)]
    rest = [copy(own.at[i], own.at[i], z_id(2 * i - 1)) for i in range(2)]
    slides(TOK // 2, TOK)
    zfwd = onward(lambda i: z_ref.at[i], z, z_id, ahead)
    norms(4)
    for load in loads:
        load.wait()
    projects((4,), [(wq_ref, q_ref), (wk_ref, k_ref), (wv_ref, v_ref)])
    for c in rest + zfwd:
        c.wait_recv()

    def place_own(h):
        for i in range(2):
            for j in range(2):
                both = jnp.concatenate(
                    [z_ref[2 * j, i].astype(F32), z_ref[2 * j + 1, i].astype(F32)], axis=0
                ).astype(BF16)
                low = D // 2 * h
                rows = slice(16 * j, 16 * (j + 1))
                pk_ref[h, y * 4 + x, i, rows, :] = both[:, low : low + D // 2]
                pv_ref[h, y * 4 + x, i, rows, :] = both[:, D + low : D + low + D // 2]

    def line(h, swap):
        buf = (pv_ref if swap else pk_ref).at[h]
        me, other = (y, x) if swap else (x, y)
        ring, ring2 = (y_id, x_id) if swap else (x_id, y_id)

        def at(i, j):
            return buf.at[i * 4 + j] if swap else buf.at[j * 4 + i]

        state = {}

        def start():
            state["one"] = spread(at(me, other), ring)
            state[0] = spread(at(me, other), ring2)

        def second(shift):
            state[shift] = spread(at(lax.rem(me + shift + 4, 4), other), ring2)

        def turn():
            state["far"] = onward(lambda i: at(i, other), me, ring, state["one"])
            second(-1)
            second(1)

        def last():
            for c in state["far"]:
                c.wait_recv()
            second(2)

        def on(shift):
            state[shift, 2] = onward(
                lambda j: at(lax.rem(me + shift + 4, 4), j), other, ring2, state[shift]
            )

        def done():
            for shift in (0, -1, 1, 2):
                for c in state[shift, 2]:
                    c.wait_recv()

        return dict(start=start, turn=turn, last=last, on=on, done=done)

    lines = [[line(h, False), line(h, True)] for h in range(2)]

    def run(h, name, *args):
        for item in lines[h]:
            item[name](*args)

    for h in range(2):
        place_own(h)
        run(h, "start")
    back4.wait_recv()
    from_up, from_down = 4 - 4 * ((z + 1) // 4), 4 * ((4 - z) // 4)
    odd = lax.rem(z, 2)
    parts = [pl.ds(TOK // 2 * i, TOK // 2) for i in range(2)]
    near = [
        [
            copy(all_ref.at[from_up, part], all_ref.at[3, part], z_id(1)),
            copy(all_ref.at[from_down, part], all_ref.at[1, part], z_id(-1)),
        ]
        for part in parts
    ]

    def two_back(i):
        for c in near[i]:
            c.wait_recv()
        return copy(
            all_ref.at[3 - 2 * odd, parts[i]], all_ref.at[2, parts[i]], z_id(1 - 2 * odd)
        )

    places()
    picks()
    run(0, "turn")
    run(1, "turn")
    norms(0)
    projects((0,), [(wk_ref, k_ref), (wv_ref, v_ref)])
    run(0, "on", 0)
    run(0, "last")
    back2 = [two_back(0)]
    suffix((0, 4), 0, 4, True, False)
    run(1, "on", 0)
    run(1, "last")
    back2.append(two_back(1))
    suffix((0, 4), 4, 8, True, False)
    run(0, "on", -1)
    run(0, "on", 1)
    norms(1)
    norms(3)
    projects((1, 3), [(wk_ref, k_ref), (wv_ref, v_ref)])
    run(1, "on", -1)
    run(1, "on", 1)
    run(0, "on", 2)
    suffix((1, 3), 4, 8, False, False)
    run(1, "on", 2)
    run(0, "done")
    prefix(0, (1, 3), False)
    for c in back2:
        c.wait_recv()
    norms(2)
    projects((2,), [(wk_ref, k_ref), (wv_ref, v_ref)])
    suffix((2,), 0, 4, False, True)
    run(1, "done")
    prefix(1, (2,), True)
    for c in used:
        c.wait_send()


def layer(slots, hid, pre, gain, bucket, rel, lens, group, wq, wk, wv):
    vmem = pl.BlockSpec(memory_space=pltpu.VMEM)
    smem = pl.BlockSpec(memory_space=pltpu.SMEM)
    hbm = pl.BlockSpec(memory_space=pl.ANY)
    pair = pltpu.VMEM((H // 2, 2 * TOK, 128), F32)
    return pl.pallas_call(
        layer_kernel,
        out_shape=jax.ShapeDtypeStruct((TOK, D), BF16),
        in_specs=[smem] + [vmem] * 7 + [hbm] * 3,
        out_specs=vmem,
        scratch_shapes=[pltpu.VMEM((D, D), BF16)] * 3
        + [
            pltpu.VMEM((8, 8, 2 * D), BF16),
            pltpu.VMEM((4, 2, 8, 2 * D), BF16),
            pltpu.VMEM((5, TOK, D), BF16),
            pltpu.VMEM((2, 16, 2, 32, D // 2), BF16),
            pltpu.VMEM((2, 16, 2, 32, D // 2), BF16),
            pltpu.VMEM((5, TOK, D), BF16),
            pltpu.VMEM((5, TOK, D), BF16),
            pltpu.VMEM((5, TOK, D), BF16),
            pltpu.VMEM((5, TOK, D), BF16),
            pltpu.VMEM((H, 1152), F32),
            pltpu.VMEM((8, TOK * H, 128), F32),
            pltpu.VMEM((4, TOK * H, 128), F32),
            pltpu.VMEM((5, TOK, 128), F32),
            pltpu.VMEM((TOK, TOK), F32),
            pair,
            pair,
            pair,
            pltpu.VMEM((2, TOK), jnp.int32),
            pltpu.SMEM((2, TOK), jnp.int32),
            pltpu.SemaphoreType.DMA((104,)),
            pltpu.SemaphoreType.DMA((104,)),
            pltpu.SemaphoreType.DMA((4,)),
        ],
        compiler_params=pltpu.CompilerParams(
            vmem_limit_bytes=58 << 20, collective_id=0, has_side_effects=True
        ),
        name="layer",
    )(slots, hid, pre, gain, bucket, rel, lens, group, wq, wk, wv)


def shards(
    hidden,
    ln_gain,
    w_query,
    w_key,
    w_value,
    w_out,
    rel_bias,
    prefix_cache,
    bucket_of_distance,
    slot_of_group,
    suffix_lengths,
    request_group,
):
    mixed = layer(
        slot_of_group,
        hidden,
        prefix_cache,
        ln_gain.reshape(8, 128),
        bucket_of_distance.reshape(8, 128),
        rel_bias.T,
        suffix_lengths,
        request_group,
        w_query,
        w_key,
        w_value,
    )
    return jnp.dot(mixed, w_out, preferred_element_type=jnp.float32).astype(jnp.bfloat16)


def solution(mesh):
    in_specs = (
        P(("grp", "tp"), None),
        P(),
        P(),
        P(),
        P(),
        P(),
        P(),
        P("grp", "tp", None, None),
        P(),
        P(),
        P("grp", None),
        P("grp", None),
    )
    out_specs = P(("grp", "tp"), None)
    return jax.shard_map(shards, mesh=mesh, in_specs=in_specs, out_specs=out_specs, check_vma=False)
```

```python
import jax
import jax.numpy as jnp
from jax import lax
from jax.experimental import pallas as pl
from jax.experimental.pallas import tpu as pltpu
from jax.sharding import PartitionSpec as P

D = 1024
H = 16
NB = 32
TOK = 128
LMAX = 512
KEYS = LMAX + TOK
PREFIX = 512
NEG = -1e30
MESH = pl.DeviceIdType.MESH
F32 = jnp.float32
BF16 = jnp.bfloat16
UNROLL = 4
NT = (((1,), (1,)), ((), ()))


def iota(shape, dim):
    return lax.broadcasted_iota(jnp.int32, shape, dim)


def layer_kernel(
    slot_ref,
    hid_ref,
    pre_ref,
    gain_ref,
    bucket_ref,
    rel_ref,
    lens_ref,
    group_ref,
    wq_hbm,
    wk_hbm,
    wv_hbm,
    out_ref,
    wq_ref,
    wk_ref,
    wv_ref,
    own_ref,
    z_ref,
    all_ref,
    pk_ref,
    pv_ref,
    n_ref,
    q_ref,
    k_ref,
    v_ref,
    rt_ref,
    s_ref,
    b_ref,
    mask_ref,
    first_ref,
    o_ref,
    top_ref,
    sum_ref,
    at_ref,
    at_smem,
    send_sem,
    recv_sem,
    load_sem,
):
    g = lax.axis_index("grp")
    t = lax.axis_index("tp")
    y, x, z = t // 16, (t // 4) % 4, t % 4

    def tp_id(i):
        return (g, lax.rem(i + 128, 64))

    def z_id(d):
        return (g, y * 16 + x * 4 + lax.rem(z + d + 4, 4))

    def x_id(d):
        return (g, y * 16 + lax.rem(x + d + 4, 4) * 4 + z)

    def y_id(d):
        return (g, lax.rem(y + d + 4, 4) * 16 + x * 4 + z)

    used = []

    def copy(src, dst, device):
        i = len(used)
        out = pltpu.make_async_remote_copy(
            src_ref=src,
            dst_ref=dst,
            send_sem=send_sem.at[i],
            recv_sem=recv_sem.at[i],
            device_id=device,
            device_id_type=MESH,
        )
        out.start()
        used.append(out)
        return out

    core = g % 2
    away = 2 - 2 * (g // 2)
    row_ids = [(away + core, t), (away + 1 - core, t), (g + 1 - 2 * core, t)]
    greet = row_ids + [tp_id(t + d) for d in (4, -4)]
    greet = greet + [ring(d) for ring in (x_id, y_id, z_id) for d in (1, -1)]
    barrier = pltpu.get_barrier_semaphore()
    for device in greet:
        pl.semaphore_signal(barrier, inc=1, device_id=device, device_id_type=MESH)

    loads = [
        pltpu.make_async_copy(src, dst, load_sem.at[i])
        for i, (src, dst) in enumerate([(wq_hbm, wq_ref), (wk_hbm, wk_ref), (wv_hbm, wv_ref)])
    ]
    for load in loads:
        load.start()

    def places():
        sub, lane = iota((TOK, TOK), 0), iota((TOK, TOK), 1)
        eye = sub == lane
        lens = jnp.sum(jnp.where(eye, lens_ref[...], 0).astype(F32), axis=1, keepdims=True)
        starts = jnp.sum(jnp.where(sub < lane, lens, 0.0), axis=0, keepdims=True)
        rows = (t * TOK + iota((TOK, 1), 0)).astype(F32)
        begun = starts <= rows
        place = rows - jnp.max(jnp.where(begun, starts, 0.0), axis=1, keepdims=True)
        req = jnp.sum(begun.astype(F32), axis=1, keepdims=True) - 1.0
        mine = lane.astype(F32) == req
        group = jnp.sum(
            jnp.where(mine, group_ref[...], 0).astype(F32), axis=1, keepdims=True
        )
        first_ref[...] = jnp.broadcast_to(group, (TOK, TOK))
        off = (PREFIX - 1) - jnp.sum(
            jnp.where(eye, place, 0.0), axis=0, keepdims=True
        ).astype(jnp.int32)
        off = jnp.clip(off, 0, PREFIX - 1)
        at_ref[...] = jnp.concatenate(
            [jnp.right_shift(off, 7), 127 - jnp.bitwise_and(off, 127)], axis=0
        )
        move = pltpu.make_async_copy(at_ref, at_smem, load_sem.at[3])
        move.start()
        row, col = iota((TOK, 128), 0), iota((TOK, 128), 1)
        low = LMAX + row - place.astype(jnp.int32)
        for j in range(5):
            at = col + 128 * j
            mask_ref[j] = jnp.where((at >= low) & (at <= LMAX + row), 0.0, NEG)
        move.wait()

    def table():
        flip = (iota((TOK, TOK), 0) + iota((TOK, TOK), 1) == TOK - 1).astype(BF16)
        bucket = jnp.dot(
            bucket_ref[...].astype(F32).astype(BF16), flip, preferred_element_type=F32
        ).astype(jnp.int32)
        for j in range(8):
            onehot = (iota((NB, 128), 0) == bucket[7 - j : 8 - j, :]).astype(F32)
            rt_ref[:, 128 * j : 128 * (j + 1)] = lax.dot_general(
                rel_ref[...],
                onehot,
                (((1,), (0,)), ((), ())),
                precision=lax.Precision.HIGHEST,
                preferred_element_type=F32,
            )
        rt_ref[:, 1024:] = jnp.zeros((H, 128), F32)

    def slides(start, stop):
        lane = iota((H, 128), 1)

        def slide(i, _):
            for a in [i * 4 + e for e in range(4)]:
                turn = jnp.bitwise_and(a + 1, 127)
                tiles = [
                    pltpu.roll(rt_ref[:, 128 * j : 128 * (j + 1)], turn, 1) for j in range(9)
                ]
                for j in range(8):
                    s_ref[j, pl.ds(pl.multiple_of(a * H, H), H), :] = jnp.where(
                        lane < a + 1, tiles[j], tiles[j + 1]
                    )
            return 0

        lax.fori_loop(start // 4, stop // 4, slide, 0)

    def picks():
        turned = s_ref.reshape(8, TOK, H, 128)
        wanted = b_ref.reshape(4, TOK, H, 128)

        def pick(i, _):
            for a in [i * 8 + e for e in range(8)]:
                for j in range(4):
                    wanted[j, a] = turned[at_smem[0, a] + j, at_smem[1, a]]
            return 0

        lax.fori_loop(0, TOK // 8, pick, 0)

    gain = jnp.concatenate([gain_ref[j : j + 1, :].astype(F32) for j in range(8)], axis=1)

    def norms(i):
        h = all_ref[i].astype(F32)
        ms = jnp.mean(h * h, axis=1, keepdims=True)
        n_ref[i] = (h * lax.rsqrt(ms + 1e-06) * gain).astype(BF16)

    def projects(blocks, pairs):
        for w_ref, dst_ref in pairs:

            def project(i, _):
                cols = pl.ds(pl.multiple_of(i * 256, 256), 256)
                n = jnp.concatenate([n_ref[b] for b in blocks], axis=0)
                r = jnp.dot(n, w_ref[:, cols], preferred_element_type=F32).astype(BF16)
                for j, b in enumerate(blocks):
                    dst_ref[b, :, cols] = r[TOK * j : TOK * (j + 1)]
                return 0

            lax.fori_loop(0, D // 256, project, 0, unroll=UNROLL)

    half = iota((TOK, 128), 1) < 64

    def stacked(cols):
        q = q_ref[4, :, cols].astype(F32)
        return jnp.concatenate([jnp.where(half, q, 0.0), jnp.where(half, 0.0, q)], axis=0)

    def gather(ref, p, tiles):
        return jnp.concatenate(
            [
                jnp.concatenate(
                    [ref[j, pl.ds(2 * p + e, TOK, stride=H), :] for j in tiles], axis=1
                )
                for e in range(2)
            ],
            axis=0,
        )

    def update(p, sets, begin, end):
        wide = (2 * TOK, 128)
        tops = [jnp.max(scores, axis=1, keepdims=True) for scores, _, _ in sets]
        top = jnp.broadcast_to(tops[0] if len(tops) == 1 else jnp.maximum(*tops), wide)
        if not begin:
            old = top_ref[p]
            top = jnp.maximum(old, top)
            scale = jnp.exp(old - top)
        total, o = 0.0, 0.0
        for scores, values, first2 in sets:
            e = jnp.exp(scores - jnp.concatenate([top] * (scores.shape[1] // 128), axis=1))
            total = total + jnp.broadcast_to(jnp.sum(e, axis=1, keepdims=True), wide)
            part = jnp.dot(e.astype(BF16), values, preferred_element_type=F32)
            if first2 is not None:
                part = jnp.where(first2, part[:, :128], part[:, 128:])
            o = o + part
        if not begin:
            total = sum_ref[p] * scale + total
            o = o_ref[p] * scale + o
        if end:
            o = o / total
            cols = pl.ds(pl.multiple_of(p * 128, 128), 128)
            out_ref[:, cols] = jnp.where(half, o[:TOK], o[TOK:]).astype(BF16)
        else:
            top_ref[p] = top
            sum_ref[p] = total
            o_ref[p] = o

    def suffix_set(p, blocks):
        cols = pl.ds(pl.multiple_of(p * 128, 128), 128)
        keys, values = [
            jnp.concatenate([ref[b, :, cols] for b in blocks], axis=0) for ref in (k_ref, v_ref)
        ]
        mask = jnp.concatenate([mask_ref[b] for b in blocks], axis=1)
        scores = (
            lax.dot_general(stacked(cols).astype(BF16), keys, NT, preferred_element_type=F32)
            + gather(s_ref, p, [b + 3 for b in blocks])
            + jnp.concatenate([mask, mask], axis=0)
        )
        return scores, values, None

    def prefix_set(p, h, i, first2):
        part = pl.ds(pl.multiple_of(i * 128, 128), 128)
        qq = stacked(pl.ds(pl.multiple_of(p * 128, 128), 128))
        qg = jnp.concatenate(
            [jnp.where(first2, qq, 0.0), jnp.where(first2, 0.0, qq)], axis=1
        ).astype(BF16)
        keys, values = [
            jnp.concatenate(
                [ref[h, :, s, :, part].reshape(PREFIX, 128) for s in range(2)], axis=1
            )
            for ref in (pk_ref, pv_ref)
        ]
        scores = lax.dot_general(qg, keys, NT, preferred_element_type=F32)
        return scores + gather(b_ref, p, range(4)), values, first2

    def suffix(blocks, start, stop, begin, end):
        def heads(p, _):
            update(p, [suffix_set(p, blocks)], begin, end)
            return 0

        lax.fori_loop(start, stop, heads, 0, unroll=UNROLL)

    def prefix(h, blocks, end):
        def heads(i, _):
            first = first_ref[...] == 0.0
            first2 = jnp.concatenate([first, first], axis=0)
            p = 4 * h + i
            sets = [prefix_set(p, h, i, first2)]
            if blocks:
                sets.append(suffix_set(p, blocks))
            update(p, sets, False, end)
            return 0

        lax.fori_loop(0, 4, heads, 0, unroll=UNROLL)

    all_ref[4] = hid_ref[...]
    mine = pl.ds(2 * g, 2)
    for i in range(2):
        raw = pre_ref[i].astype(F32)
        own_ref[2 * g + i] = jnp.concatenate([raw[:, 0, :], raw[:, 1, :]], axis=1).astype(BF16)
    pl.semaphore_wait(barrier, len(greet))

    rows = [copy(own_ref.at[mine], own_ref.at[mine], device) for device in row_ids]
    back4 = copy(hid_ref, all_ref.at[0], tp_id(t + 4))
    table()
    slides(0, TOK // 2)
    for c in rows:
        c.wait_recv()
    for i in range(2):
        z_ref[z, i] = own_ref[slot_ref[2 * g + i]]

    def spread(part, ring):
        return [copy(part, part, ring(1)), copy(part, part, ring(-1))]

    def onward(part, me, ring, first):
        out = []
        for i, step in ((0, 1), (1, -1)):
            first[i].wait_recv()
            piece = part(lax.rem(me - step + 4, 4)).at[i]
            out.append(copy(piece, piece, ring(step)))
        return out

    own = z_ref.at[z]
    ahead = [copy(own.at[i], own.at[i], z_id(1 - 2 * i)) for i in range(2)]
    rest = [copy(own.at[i], own.at[i], z_id(2 * i - 1)) for i in range(2)]
    slides(TOK // 2, TOK)
    zfwd = onward(lambda i: z_ref.at[i], z, z_id, ahead)
    norms(4)
    for load in loads:
        load.wait()
    projects((4,), [(wq_ref, q_ref), (wk_ref, k_ref), (wv_ref, v_ref)])
    for c in rest + zfwd:
        c.wait_recv()

    def place_own(h):
        for i in range(2):
            for j in range(2):
                both = jnp.concatenate(
                    [z_ref[2 * j, i].astype(F32), z_ref[2 * j + 1, i].astype(F32)], axis=0
                ).astype(BF16)
                low = D // 2 * h
                rows = slice(16 * j, 16 * (j + 1))
                pk_ref[h, y * 4 + x, i, rows, :] = both[:, low : low + D // 2]
                pv_ref[h, y * 4 + x, i, rows, :] = both[:, D + low : D + low + D // 2]

    def line(h, swap):
        buf = (pv_ref if swap else pk_ref).at[h]
        me, other = (y, x) if swap else (x, y)
        ring, ring2 = (y_id, x_id) if swap else (x_id, y_id)

        def at(i, j):
            return buf.at[i * 4 + j] if swap else buf.at[j * 4 + i]

        state = {}

        def start():
            state["one"] = spread(at(me, other), ring)
            state[0] = spread(at(me, other), ring2)

        def second(shift):
            state[shift] = spread(at(lax.rem(me + shift + 4, 4), other), ring2)

        def turn():
            state["far"] = onward(lambda i: at(i, other), me, ring, state["one"])
            second(-1)
            second(1)

        def last():
            for c in state["far"]:
                c.wait_recv()
            second(2)

        def on(shift):
            state[shift, 2] = onward(
                lambda j: at(lax.rem(me + shift + 4, 4), j), other, ring2, state[shift]
            )

        def done():
            for shift in (0, -1, 1, 2):
                for c in state[shift, 2]:
                    c.wait_recv()

        return dict(start=start, turn=turn, last=last, on=on, done=done)

    lines = [[line(h, False), line(h, True)] for h in range(2)]

    def run(h, name, *args):
        for item in lines[h]:
            item[name](*args)

    for h in range(2):
        place_own(h)
        run(h, "start")
    back4.wait_recv()
    from_up, from_down = 4 - 4 * ((z + 1) // 4), 4 * ((4 - z) // 4)
    odd = lax.rem(z, 2)
    parts = [pl.ds(TOK // 2 * i, TOK // 2) for i in range(2)]
    near = [
        [
            copy(all_ref.at[from_up, part], all_ref.at[3, part], z_id(1)),
            copy(all_ref.at[from_down, part], all_ref.at[1, part], z_id(-1)),
        ]
        for part in parts
    ]

    def two_back(i):
        for c in near[i]:
            c.wait_recv()
        return copy(
            all_ref.at[3 - 2 * odd, parts[i]], all_ref.at[2, parts[i]], z_id(1 - 2 * odd)
        )

    places()
    picks()
    run(0, "turn")
    run(1, "turn")
    norms(0)
    projects((0,), [(wk_ref, k_ref), (wv_ref, v_ref)])
    run(0, "on", 0)
    run(0, "last")
    back2 = [two_back(0)]
    suffix((0, 4), 0, 4, True, False)
    run(1, "on", 0)
    run(1, "last")
    back2.append(two_back(1))
    suffix((0, 4), 4, 8, True, False)
    run(0, "on", -1)
    run(0, "on", 1)
    norms(1)
    norms(3)
    projects((1, 3), [(wk_ref, k_ref), (wv_ref, v_ref)])
    run(1, "on", -1)
    run(1, "on", 1)
    run(0, "on", 2)
    suffix((1, 3), 4, 8, False, False)
    run(1, "on", 2)
    run(0, "done")
    prefix(0, (1, 3), False)
    for c in back2:
        c.wait_recv()
    norms(2)
    projects((2,), [(wk_ref, k_ref), (wv_ref, v_ref)])
    suffix((2,), 0, 4, False, True)
    run(1, "done")
    prefix(1, (2,), True)
    for c in used:
        c.wait_send()


def layer(slots, hid, pre, gain, bucket, rel, lens, group, wq, wk, wv):
    vmem = pl.BlockSpec(memory_space=pltpu.VMEM)
    smem = pl.BlockSpec(memory_space=pltpu.SMEM)
    hbm = pl.BlockSpec(memory_space=pl.ANY)
    pair = pltpu.VMEM((H // 2, 2 * TOK, 128), F32)
    return pl.pallas_call(
        layer_kernel,
        out_shape=jax.ShapeDtypeStruct((TOK, D), BF16),
        in_specs=[smem] + [vmem] * 7 + [hbm] * 3,
        out_specs=vmem,
        scratch_shapes=[pltpu.VMEM((D, D), BF16)] * 3
        + [
            pltpu.VMEM((8, 8, 2 * D), BF16),
            pltpu.VMEM((4, 2, 8, 2 * D), BF16),
            pltpu.VMEM((5, TOK, D), BF16),
            pltpu.VMEM((2, 16, 2, 32, D // 2), BF16),
            pltpu.VMEM((2, 16, 2, 32, D // 2), BF16),
            pltpu.VMEM((5, TOK, D), BF16),
            pltpu.VMEM((5, TOK, D), BF16),
            pltpu.VMEM((5, TOK, D), BF16),
            pltpu.VMEM((5, TOK, D), BF16),
            pltpu.VMEM((H, 1152), F32),
            pltpu.VMEM((8, TOK * H, 128), F32),
            pltpu.VMEM((4, TOK * H, 128), F32),
            pltpu.VMEM((5, TOK, 128), F32),
            pltpu.VMEM((TOK, TOK), F32),
            pair,
            pair,
            pair,
            pltpu.VMEM((2, TOK), jnp.int32),
            pltpu.SMEM((2, TOK), jnp.int32),
            pltpu.SemaphoreType.DMA((104,)),
            pltpu.SemaphoreType.DMA((104,)),
            pltpu.SemaphoreType.DMA((4,)),
        ],
        compiler_params=pltpu.CompilerParams(
            vmem_limit_bytes=58 << 20, collective_id=0, has_side_effects=True
        ),
        name="layer",
    )(slots, hid, pre, gain, bucket, rel, lens, group, wq, wk, wv)


def shards(
    hidden,
    ln_gain,
    w_query,
    w_key,
    w_value,
    w_out,
    rel_bias,
    prefix_cache,
    bucket_of_distance,
    slot_of_group,
    suffix_lengths,
    request_group,
):
    mixed = layer(
        slot_of_group,
        hidden,
        prefix_cache,
        ln_gain.reshape(8, 128),
        bucket_of_distance.reshape(8, 128),
        rel_bias.T,
        suffix_lengths,
        request_group,
        w_query,
        w_key,
        w_value,
    )
    return jnp.dot(mixed, w_out, preferred_element_type=jnp.float32).astype(jnp.bfloat16)


def solution(mesh):
    in_specs = (
        P(("grp", "tp"), None),
        P(),
        P(),
        P(),
        P(),
        P(),
        P(),
        P("grp", "tp", None, None),
        P(),
        P(),
        P("grp", None),
        P("grp", None),
    )
    out_specs = P(("grp", "tp"), None)
    return jax.shard_map(shards, mesh=mesh, in_specs=in_specs, out_specs=out_specs, check_vma=False)
```
